128 devices in a mesh: wide: 16 (over z, x), narrow: 8 (over y, core).
Axes of the slice: x: 4, y: 4, z: 4, core: 2. Of those that a mesh axis runs over, the one named last changes fastest.
Arguments:
- positions: float32 [3, 6291456], P(None, ('wide', 'narrow')), may hold values from -6 to 6
- velocities: float32 [3, 6291456], P(None, ('wide', 'narrow')), may hold values from -6 to 6
- nodal_mass: float32 [6291456], P(('wide', 'narrow')), may hold values from 0.5 to 2
- thickness: float32 [6291456], P(('wide', 'narrow')), may hold values from 0.05 to 0.3
- pack_index: int32 [128, 65536], P(('wide', 'narrow')), may hold values from 0 to 49152, as said below
- connectivity: int32 [262144, 4], P(('wide', 'narrow')), may hold values from 0 to 65535, as said below
- tile_list: int32 [2, 131072], P(None, ('wide', 'narrow')), may hold values from 0 to 511, as said below
- pair_mask: int32 [131072, 256], P(('wide', 'narrow')), may hold values 0 or 1
- tile_count: int32 [128], P(('wide', 'narrow')), may hold values from 256 to 1024
Outputs:
- contact_force: float32 [3, 6291456], P(None, ('wide', 'narrow'))
The draws below stay inside these ranges and needn't reach their ends.
Inputs may be any that keep to these rules, and one draw needn't show every extreme that they name: `pack_index`: row s lists, for each send slot p * 512 + k of mesh owner s (bound for partition p), the local node it carries, or 49152 for an empty slot. Each of the 49152 local nodes appears exactly once in its row; every block of 512 slots carries at least 128 nodes, and in every row one block is full. `connectivity`: rows p * 2048 to (p + 1) * 2048 - 1 are partition p's segments; each entry is a non-empty slot of contact_state[p], and the 8192 entries of one partition are distinct. `tile_list`: row 0 holds node blocks below 512, row 1 segment blocks below 24. Within one partition's 1024 entries the first 512 node blocks are distinct and entry t + 512 has the node block of entry t.
All inputs are finite; a program needn't handle non-finite values. No bound on the sum of `pair_mask` on one device may be relied on, other than what follows from the above.
Results may differ from the reference program's by a relative error of at most 0.0003.
Values sent between devices are 32-bit elements; how exact they have to be, the bound alone decides.
A program may use at most 128 MiB of HBM per device.

```python
import math
import jax
import jax.numpy as jnp
from jax import lax

NODE_DEV = 49152
SEG_DEV = 2048
TILE_SEGS = 256
PARTITIONS = 128
CAP = 512
SLOTS = 65536
NODE_BLOCKS = 512
TILE_CAP = 1024
GHOST = 512
SEG_BLOCKS = 24
NODES = 6291456
N_WIDE = 16
N_NARROW = 8


def build_pack(key):
    base = jax.random.fold_in(key, 7)

    def one_source(source):
        source_key = jax.random.fold_in(base, source)
        key_rank, key_order, key_node = jax.random.split(source_key, 3)
        ranks = jax.random.permutation(key_rank, jnp.tile(jnp.arange(CAP, dtype=jnp.int32), (PARTITIONS, 1)), axis=1, independent=True)
        full_block = (5 * source + 3) % PARTITIONS
        blocks = jnp.arange(PARTITIONS, dtype=jnp.int32)[:, None]
        tier = jnp.where(blocks == full_block, 2, jnp.where(ranks < CAP // 4, 1, 0))
        last_slot = (source == PARTITIONS - 1) & (jnp.arange(CAP, dtype=jnp.int32)[None, :] == CAP - 1)
        tier = jnp.where(last_slot, 2, tier)
        order = jax.random.permutation(key_order, SLOTS).astype(jnp.int32)
        score = tier.reshape(-1).astype(jnp.int32) * SLOTS + order
        chosen = jnp.argsort(-score)[:NODE_DEV]
        nodes = jax.random.permutation(key_node, NODE_DEV).astype(jnp.int32)
        return jnp.full((SLOTS,), NODE_DEV, jnp.int32).at[chosen].set(nodes)
    return jax.vmap(one_source)(jnp.arange(PARTITIONS, dtype=jnp.int32))


def draw_pack_index(key, part):
    return build_pack(key)


def draw_connectivity(key, part):
    pack = build_pack(key)
    base = jax.random.fold_in(key, 13)

    def one_partition(partition):
        received = lax.dynamic_slice_in_dim(pack, partition * CAP, CAP, 1).reshape(-1)
        filled = (received < NODE_DEV).astype(jnp.int32)
        order = jax.random.permutation(jax.random.fold_in(base, partition), SLOTS).astype(jnp.int32)
        last_one = (jnp.arange(SLOTS, dtype=jnp.int32) == SLOTS - 1).astype(jnp.int32)
        score = filled * (2 * SLOTS) + last_one * SLOTS + order
        chosen = jnp.argsort(-score)[:4 * SEG_DEV]
        return chosen.astype(jnp.int32).reshape(SEG_DEV, 4)
    return jax.vmap(one_partition)(jnp.arange(PARTITIONS, dtype=jnp.int32)).reshape(-1, 4)


def draw_tile_list(key, part):
    base = jax.random.fold_in(key, 17)

    def one_partition(partition):
        key_node, key_seg = jax.random.split(jax.random.fold_in(base, partition))
        node_order = jax.random.permutation(key_node, NODE_BLOCKS).astype(jnp.int32)
        node_rows = jnp.tile(node_order, TILE_CAP // NODE_BLOCKS)
        seg_rows = jax.random.randint(key_seg, (TILE_CAP,), 0, SEG_BLOCKS, dtype=jnp.int32)
        return jnp.stack([node_rows, seg_rows])
    stacked = jax.vmap(one_partition)(jnp.arange(PARTITIONS, dtype=jnp.int32))
    return jnp.transpose(stacked, (1, 0, 2)).reshape(2, -1)


def draw_tile_count(key, part):
    key_count, key_pick = jax.random.split(jax.random.fold_in(key, 19))
    counts = jax.random.randint(key_count, (PARTITIONS,), NODE_BLOCKS // 2, NODE_BLOCKS + 1, dtype=jnp.int32)
    busiest = jax.random.randint(key_pick, (), 0, PARTITIONS, dtype=jnp.int32)
    lightest = (busiest + PARTITIONS // 2) % PARTITIONS
    counts = counts.at[busiest].set(TILE_CAP)
    return counts.at[lightest].set(NODE_BLOCKS // 2)


def place_ends(values, key, low, high):
    dims = values.shape
    spot = [jax.random.randint(jax.random.fold_in(key, axis), (), 0, dims[axis]) for axis in range(len(dims))]
    values = values.at[tuple(spot)].set(low)
    longest = dims.index(max(dims))
    spot[longest] = (spot[longest] + 1) % dims[longest]
    return values.at[tuple(spot)].set(high)


def levels(key, extent, cuts, low, high):
    loudness = 1.0
    for axis_at, shards_of in cuts:
        steps = jax.random.uniform(jax.random.fold_in(jax.random.fold_in(key, 6), axis_at), (shards_of,), jnp.float32, low / len(cuts), high / len(cuts))
        loudness = loudness * jnp.repeat(jnp.exp(steps), extent[axis_at] // shards_of).reshape((-1,) + (1,) * (len(extent) - 1 - axis_at))
    return loudness


def scatter_about(own_key, dims, scale, reach, shards=(), held_as=jnp.bfloat16):
    factor_of = levels(own_key, dims, shards, -0.22, 0.18) if shards else 1.0
    drawn = jax.random.normal(own_key, dims, jnp.float32) * scale * factor_of
    return jnp.minimum(jnp.maximum(drawn, -reach), reach).astype(held_as)


def setup_inputs(seed: int = 0) -> dict:
    streams_of = jax.random.split(jax.random.key(seed), 10)
    positions = scatter_about(streams_of[0], (3, NODES), 1.0, 6.0, ((1, 128),), jnp.float32)
    velocities = scatter_about(streams_of[1], (3, NODES), 1.0, 6.0, ((1, 128),), jnp.float32)
    nodal_mass = jnp.clip(jnp.exp(math.log(2.0) - 1.3862944 * jax.random.uniform(streams_of[2], (NODES,), jnp.float32) ** levels(streams_of[2], (NODES,), ((0, 128),), -0.2, 0.2)), 0.5, 2.0)
    thickness = jnp.clip(0.05 + 0.25 * jax.random.uniform(streams_of[3], (NODES,), jnp.float32) ** levels(streams_of[3], (NODES,), ((0, 128),), -0.2, 0.2), 0.05, 0.3)
    pack_index = draw_pack_index(jax.random.fold_in(streams_of[9], 71), 0)
    connectivity = draw_connectivity(jax.random.fold_in(streams_of[9], 71), 0)
    tile_list = draw_tile_list(jax.random.fold_in(streams_of[9], 71), 0)
    pair_mask = place_ends((jax.random.randint(streams_of[7], (PARTITIONS * TILE_CAP, TILE_SEGS), 0, 2) < 1).astype(jnp.int32), jax.random.fold_in(streams_of[7], 1), 0, 1)
    tile_count = draw_tile_count(jax.random.fold_in(streams_of[9], 71), 0)
    return {"positions": positions, "velocities": velocities, "nodal_mass": nodal_mass, "thickness": thickness, "pack_index": pack_index, "connectivity": connectivity, "tile_list": tile_list, "pair_mask": pair_mask, "tile_count": tile_count}


stiffness = 1.0
damping = 0.3
tiles_per_turn = 32

def quad_features(quad_nodes):
    corner = quad_nodes[:, 0:3]
    motion = quad_nodes[:, 3:6]
    centre = (corner[0] + corner[1] + corner[2] + corner[3]) * 0.25
    diag_one = corner[2] - corner[0]
    diag_two = corner[3] - corner[1]
    cross_raw = jnp.stack([diag_one[1] * diag_two[2] - diag_one[2] * diag_two[1], diag_one[2] * diag_two[0] - diag_one[0] * diag_two[2], diag_one[0] * diag_two[1] - diag_one[1] * diag_two[0]])
    length = jnp.sqrt(lax.optimization_barrier(jnp.sum(cross_raw * cross_raw, axis=0)))
    normal = cross_raw / jnp.maximum(length, 1.0)
    drift = (motion[0] + motion[1] + motion[2] + motion[3]) * 0.25
    spread = lax.optimization_barrier(jnp.sum((corner - centre[None]) ** 2, axis=(0, 1))) * 0.25
    return jnp.concatenate([centre, normal, drift, spread[None]], axis=0)

def ghost_block(ghost_rim):
    flat = ghost_rim.reshape(9, ghost_rim.shape[2], ghost_rim.shape[3])
    chosen = jnp.take(flat, jnp.array([0, 1, 2, 3, 5, 6, 7, 8], dtype=jnp.int32), axis=0)
    return jnp.transpose(chosen, (1, 0, 2)).reshape(flat.shape[1], -1)

def pair_forces(node_tile, seg_tile, mask_tile):
    position = node_tile[0:3, :, :, None]
    centre = seg_tile[0:3, :, None, :]
    normal = seg_tile[3:6, :, None, :]
    signed_gap = lax.optimization_barrier(jnp.sum(position * normal, axis=0)) - lax.optimization_barrier(jnp.sum(centre * normal, axis=0)) - node_tile[7][:, :, None]
    intersection = jnp.maximum(-signed_gap, 0.0)
    distance = lax.optimization_barrier(jnp.sum((position - centre) ** 2, axis=0))
    weight = jnp.exp(-distance / (seg_tile[9][:, None, :] + 0.25)) * mask_tile[:, None, :]
    closing = lax.optimization_barrier(jnp.sum((node_tile[3:6, :, :, None] - seg_tile[6:9, :, None, :]) * normal, axis=0))
    magnitude = intersection * weight * (stiffness * node_tile[6][:, :, None] - damping * closing)
    return lax.optimization_barrier(jnp.sum(magnitude[None] * normal, axis=3))

def contact_pass(arrived, seg_all, tile_rows, mask_rows, tile_total):
    block_count = arrived.shape[1] // 128
    node_blocks = arrived.reshape(arrived.shape[0], block_count, 128)
    seg_blocks = seg_all.reshape(seg_all.shape[0], seg_all.shape[1] // 256, 256)
    turns = (tile_total + tiles_per_turn - 1) // tiles_per_turn

    def one_turn(turn_index, totals):
        first_tile = (turn_index * tiles_per_turn).astype(jnp.int32)
        chosen = lax.dynamic_slice_in_dim(tile_rows, first_tile, tiles_per_turn, 1)
        mask_tile = lax.dynamic_slice_in_dim(mask_rows, first_tile, tiles_per_turn, 0).astype(arrived.dtype)
        node_tile = jnp.take(node_blocks, chosen[0], axis=1)
        seg_tile = jnp.take(seg_blocks, chosen[1], axis=1)
        live_tiles = (first_tile + jnp.arange(tiles_per_turn, dtype=jnp.int32) < tile_total).astype(arrived.dtype)
        tile_force = pair_forces(node_tile, seg_tile, mask_tile) * live_tiles[None, :, None]
        return totals.at[:, chosen[0], :].add(tile_force)
    totals = lax.fori_loop(0, turns, one_turn, jnp.zeros((3, block_count, 128), arrived.dtype))
    return totals.reshape(3, -1)

def node_state(partition, node_data, pack_index):
    owners = N_WIDE * N_NARROW
    local = lax.dynamic_slice_in_dim(pack_index, (partition * CAP).astype(jnp.int32), CAP, 1)
    offsets = jnp.arange(owners, dtype=jnp.int32)[:, None] * NODE_DEV
    valid = local < NODE_DEV
    target = jnp.where(valid, offsets + local, 0).reshape(-1)
    gathered = jnp.take(node_data, target, axis=1)
    return gathered * valid.reshape(-1).astype(node_data.dtype)[None, :]

def reference(positions, velocities, nodal_mass, thickness, pack_index, connectivity, tile_list, pair_mask, tile_count):
    owners = N_WIDE * N_NARROW
    node_data = jnp.concatenate([positions, velocities, nodal_mass[None], thickness[None]], axis=0)
    every = jnp.arange(owners, dtype=jnp.int32)

    def seg_features(partition):
        state = node_state(partition, node_data, pack_index)
        corners = lax.dynamic_slice_in_dim(connectivity, (partition * SEG_DEV).astype(jnp.int32), SEG_DEV, 0)
        quad_nodes = jnp.transpose(jnp.take(state[0:6], corners, axis=1), (2, 0, 1))
        return quad_features(quad_nodes)
    features = lax.map(seg_features, every)
    grid = features[:, :, :GHOST].reshape(N_WIDE, N_NARROW, 10, GHOST)
    padded = jnp.pad(grid, ((1, 1), (1, 1), (0, 0), (0, 0)))

    def partition_forces(partition):
        state = node_state(partition, node_data, pack_index)
        row_index = (partition // N_NARROW).astype(jnp.int32)
        column_index = (partition % N_NARROW).astype(jnp.int32)
        zero_index = jnp.zeros((), jnp.int32)
        ghost_rim = lax.dynamic_slice(padded, (row_index, column_index, zero_index, zero_index), (3, 3, 10, GHOST))
        seg_all = jnp.concatenate([features[partition], ghost_block(ghost_rim)], axis=1)
        first_entry = (partition * TILE_CAP).astype(jnp.int32)
        tile_rows = lax.dynamic_slice_in_dim(tile_list, first_entry, TILE_CAP, 1)
        mask_rows = lax.dynamic_slice_in_dim(pair_mask, first_entry, TILE_CAP, 0)
        return contact_pass(state, seg_all, tile_rows, mask_rows, tile_count[partition])
    slot_force = lax.map(partition_forces, every)
    values = jnp.transpose(slot_force.reshape(owners, 3, owners, CAP), (1, 2, 0, 3)).reshape(3, -1)
    offsets = jnp.arange(owners, dtype=jnp.int32)[:, None] * NODE_DEV
    target = jnp.where(pack_index < NODE_DEV, offsets + pack_index, owners * NODE_DEV).reshape(-1)
    result = jnp.zeros((3, owners * NODE_DEV), slot_force.dtype)
    return result.at[:, target].set(values, mode='drop')
```

```python
import functools
import jax
import jax.numpy as jnp
from jax import lax
from jax.experimental import pallas as pl
from jax.experimental.pallas import tpu as pltpu
from jax.sharding import PartitionSpec as P

F32 = jnp.float32
BF16 = jnp.bfloat16
I32 = jnp.int32
CHUNK = 256
LOG2E = 1.4426950408889634


def iota(shape, axis):
    return lax.broadcasted_iota(I32, shape, axis)


def split3(x):
    high = x.astype(BF16)
    rest = x - high.astype(F32)
    middle = rest.astype(BF16)
    low = (rest - middle.astype(F32)).astype(BF16)
    return high, middle, low


def expand_rows(tile):
    rows = tile.shape[0]
    high, middle, low = split3(tile)
    parts = [high.astype(F32), middle.astype(F32), low.astype(F32)]
    stacked = jnp.concatenate(parts, axis=0).astype(BF16)
    spread = (iota((3 * rows, 128), 0) % rows == iota((3 * rows, 128), 1) % 8).astype(F32).astype(BF16)
    return lax.dot_general(stacked, spread, (((0,), (0,)), ((), ())), preferred_element_type=F32)


def merge_groups(rows, shape):
    lane = iota(shape, 1)
    bit = 8
    while len(rows) > 1:
        odd = (lane & bit) != 0
        rows = [jnp.where(odd, rows[2 * i + 1], rows[2 * i]) for i in range(len(rows) // 2)]
        bit *= 2
    return rows[0]


def feature_major(rows):
    lane = iota((8, 128), 1)
    pick = (lane // 8) * 8 + iota((8, 128), 0)
    out = None
    for r in range(8):
        moved = jnp.take_along_axis(rows[r], pick, axis=1)
        out = moved if out is None else jnp.where(lane % 8 == r, moved, out)
    return out


def index_chunks(index_ref, body):
    def turn(i, carry):
        body(i, lambda k: index_ref[0, i * CHUNK + k])
        return carry

    lax.fori_loop(0, index_ref.shape[1] // CHUNK, turn, 0, unroll=2)


def pack_kernel(index_ref, pos_ref, vel_ref, mass_ref, thick_ref, out_ref, rows_ref):
    nodes = pos_ref.shape[1]

    def fill(b, carry):
        at = pl.ds(pl.multiple_of(b * 128, 128), 128)
        tile = jnp.concatenate([pos_ref[:, at], vel_ref[:, at], mass_ref[:, at], thick_ref[:, at]], axis=0)
        rows_ref[at, :] = expand_rows(tile)
        return carry

    lax.fori_loop(0, nodes // 128, fill, 0, unroll=8)
    rows_ref[nodes : nodes + 8, :] = jnp.zeros((8, 128), F32)

    def chunk(c, index):
        for half in range(CHUNK // 128):
            lines = []
            for r in range(8):
                got = [
                    rows_ref[pl.ds(index(half * 128 + k * 8 + r), 8, stride=0), :] for k in range(16)
                ]
                lines.append(merge_groups(got, (8, 128)))
            out_ref[c * (CHUNK // 128) + half] = feature_major(lines)

    index_chunks(index_ref, chunk)


VMEM = pl.BlockSpec(memory_space=pltpu.VMEM)
SMEM = pl.BlockSpec(memory_space=pltpu.SMEM)


def pack(positions, velocities, nodal_mass, thickness, pack_index):
    nodes = positions.shape[1]
    return pl.pallas_call(
        pack_kernel,
        out_shape=jax.ShapeDtypeStruct((pack_index.shape[1] // 128, 8, 128), F32),
        in_specs=[SMEM, VMEM, VMEM, VMEM, VMEM],
        out_specs=VMEM,
        scratch_shapes=[
            pltpu.VMEM((nodes + 8, 128), F32),
        ],
        compiler_params=pltpu.CompilerParams(vmem_limit_bytes=48 << 20),
        name="pack",
    )(pack_index, positions, velocities, nodal_mass.reshape(1, -1), thickness.reshape(1, -1))


def scatter_kernel(index_ref, force_ref, out_ref, rows_ref, ex_a, ex_b):
    nodes = out_ref.shape[1]

    def chunk(c, index):
        for half, ex in enumerate((ex_a, ex_b)):
            ex[...] = expand_rows(force_ref[c * 2 + half])
            for j in range(128):
                rows_ref[pl.ds(index(half * 128 + j), 1), :] = ex[j : j + 1, :]

    index_chunks(index_ref, chunk)

    def collect(b, carry):
        at = pl.multiple_of(b * 128, 128)
        tiles = [rows_ref[pl.ds(at + k * 8, 8), :] for k in range(16)]
        merged = merge_groups(tiles, (8, 128))
        lines = [jnp.broadcast_to(merged[r : r + 1], (8, 128)) for r in range(8)]
        out_ref[:, pl.ds(at, 128)] = feature_major(lines)[0:3]
        return carry

    lax.fori_loop(0, nodes // 128, collect, 0, unroll=4)


def scatter(force, pack_index, nodes):
    return pl.pallas_call(
        scatter_kernel,
        out_shape=jax.ShapeDtypeStruct((3, nodes), F32),
        in_specs=[SMEM, VMEM],
        out_specs=VMEM,
        scratch_shapes=[
            pltpu.VMEM((nodes + 8, 128), F32),
            pltpu.VMEM((128, 128), F32),
            pltpu.VMEM((128, 128), F32),
        ],
        compiler_params=pltpu.CompilerParams(vmem_limit_bytes=48 << 20),
        name="scatter",
    )(pack_index, force)


def features_kernel(conn_ref, state_ref, out_ref):
    lane = iota((8, 128), 1)

    def chunk(c, carry):
        corner = []
        for i in range(4):
            found = jnp.zeros((8, 128), F32)
            for q in range(128):
                slot = conn_ref[i, c * 128 + q]
                tile = state_ref[slot >> 7]
                moved = pltpu.roll(tile, (q - slot) & 127, axis=1)
                found = jnp.where(lane == q, moved, found)
            corner.append(found)
        total = (corner[0] + corner[1] + corner[2] + corner[3]) * 0.25
        centre = total[0:3]
        d1 = corner[2] - corner[0]
        d2 = corner[3] - corner[1]
        w0 = d1[1:2] * d2[2:3] - d1[2:3] * d2[1:2]
        w1 = d1[2:3] * d2[0:1] - d1[0:1] * d2[2:3]
        w2 = d1[0:1] * d2[1:2] - d1[1:2] * d2[0:1]
        scale = jnp.maximum(jnp.sqrt(w0 * w0 + w1 * w1 + w2 * w2), 1.0)
        off = [corner[i][0:3] - centre for i in range(4)]
        square = off[0] * off[0] + off[1] * off[1] + off[2] * off[2] + off[3] * off[3]
        spread = (square[0:1] + square[1:2] + square[2:3]) * 0.25
        at = pl.ds(pl.multiple_of(c * 128, 128), 128)
        out_ref[0:3, at] = centre
        out_ref[3:6, at] = jnp.concatenate([w0 / scale, w1 / scale, w2 / scale], axis=0)
        out_ref[6:9, at] = total[3:6]
        out_ref[9:10, at] = spread
        return carry

    lax.fori_loop(0, out_ref.shape[1] // 128, chunk, 0)


def features(connectivity, state):
    segs = connectivity.shape[0]
    return pl.pallas_call(
        features_kernel,
        out_shape=jax.ShapeDtypeStruct((10, segs), F32),
        in_specs=[SMEM, VMEM],
        out_specs=VMEM,
        compiler_params=pltpu.CompilerParams(vmem_limit_bytes=16 << 20),
        name="features",
    )(connectivity.T, state)


def contact_kernel(tiles_ref, count_ref, state_ref, seg_ref, mask_ref, out_ref, coef_ref, normal_ref, *, stiffness, damping):
    blocks = state_ref.shape[0]
    seg_blocks = seg_ref.shape[1] // 256
    out_ref[...] = jnp.zeros_like(out_ref)

    def stack_seg(rows):
        zero = jnp.zeros((1, 256), F32)
        block = jnp.concatenate([zero if r is None else r for r in rows] + [zero] * (16 - len(rows)), axis=0)
        high, middle, low = split3(block)
        return jnp.concatenate([high, high, high, middle, middle, low], axis=0)

    def prepare(s, carry):
        f = seg_ref[:, pl.ds(pl.multiple_of(s * 256, 256), 256)]
        c = [f[i : i + 1] for i in range(3)]
        n = [f[i : i + 1] for i in range(3, 6)]
        u = [f[i : i + 1] for i in range(6, 9)]
        rate = LOG2E / (f[9:10] + 0.25)
        one = jnp.ones((1, 256), F32)
        dot = lambda a, b: a[0] * b[0] + a[1] * b[1] + a[2] * b[2]
        depth = [-n[0], -n[1], -n[2], None, None, None, None, one, None, dot(c, n)]
        power = [2.0 * rate * c[0], 2.0 * rate * c[1], 2.0 * rate * c[2], None, None, None, None, None, -rate, -rate * dot(c, c)]
        push = [None, None, None, -damping * n[0], -damping * n[1], -damping * n[2], stiffness * one, None, None, damping * dot(u, n)]
        coef_ref[s, 0] = stack_seg(depth)
        coef_ref[s, 1] = stack_seg(power)
        coef_ref[s, 2] = stack_seg(push)
        high, middle, _ = split3(f[3:6])
        normal_ref[s] = jnp.concatenate([high.astype(F32), middle.astype(F32), jnp.zeros((2, 256), F32)], axis=0)
        return carry

    lax.fori_loop(0, seg_blocks, prepare, 0)
    total = count_ref[0]
    row = iota((8, 128), 0)

    def tile_pair(t, carry):
        block = tiles_ref[0, t]
        node = state_ref[block]
        sq = jnp.sum(jnp.where(row < 3, node * node, 0.0), axis=0, keepdims=True)
        extra = jnp.where(row == 0, sq, jnp.where(row == 1, 1.0, 0.0))
        high, middle, low = split3(jnp.concatenate([node, extra], axis=0))
        nodes = jnp.concatenate([high, middle, low, high, middle, high], axis=0).T
        force = jnp.zeros((8, 128), F32)
        for half in range(2):
            e = t + half * blocks
            s = tiles_ref[1, e]
            live = (e < total).astype(F32)
            term = [
                jnp.dot(nodes, coef_ref[s, i], preferred_element_type=F32) for i in range(3)
            ]
            size = jnp.maximum(term[0], 0.0) * jnp.exp2(term[1]) * term[2]
            top = size.astype(BF16)
            rest = (size - top.astype(F32)).astype(BF16)
            mask = mask_ref[pl.ds(e, 1), :].astype(F32) * live
            weights = (normal_ref[s] * mask).astype(BF16)
            for part in (top, rest):
                force += lax.dot_general(weights, part, (((1,), (1,)), ((), ())), preferred_element_type=F32)
        out_ref[block, 0:3] = force[0:3] + force[3:6]
        return carry

    lax.fori_loop(0, jnp.minimum(total, blocks), tile_pair, 0)


def contact(state, seg_all, tile_list, pair_mask, tile_count, stiffness, damping):
    blocks = state.shape[0]
    seg_blocks = seg_all.shape[1] // 256
    return pl.pallas_call(
        functools.partial(contact_kernel, stiffness=stiffness, damping=damping),
        out_shape=jax.ShapeDtypeStruct((blocks, 4, 128), F32),
        in_specs=[SMEM, SMEM, VMEM, VMEM, VMEM],
        out_specs=VMEM,
        scratch_shapes=[
            pltpu.VMEM((seg_blocks, 3, 96, 256), BF16),
            pltpu.VMEM((seg_blocks, 8, 256), F32),
        ],
        compiler_params=pltpu.CompilerParams(vmem_limit_bytes=32 << 20),
        name="contact",
    )(tile_list, tile_count, state, seg_all, pair_mask)


STIFFNESS = 1.0
DAMPING = 0.3
AXES = ("wide", "narrow")


def swap(blocks):
    return lax.all_to_all(blocks, AXES, split_axis=0, concat_axis=0, tiled=True)


def padded(cells, sides):
    for axis, dim in sides:
        ends = lax.axis_size(axis) - 1
        head = lax.slice_in_dim(cells, 0, 1, axis=dim)
        tail = lax.slice_in_dim(cells, cells.shape[dim] - 1, cells.shape[dim], axis=dim)
        before = lax.ppermute(tail, axis, [(i, i + 1) for i in range(ends)])
        after = lax.ppermute(head, axis, [(i + 1, i) for i in range(ends)])
        cells = jnp.concatenate([before, cells, after], axis=dim)
    return cells


def on_device(positions, velocities, nodal_mass, thickness, pack_index, connectivity, tile_list, pair_mask, tile_count):
    state = swap(pack(positions, velocities, nodal_mass, thickness, pack_index))
    own = features(connectivity, state)
    ghosts = connectivity.shape[0] // 4
    rim = padded(own[None, None, :, :ghosts], (("wide", 0), ("narrow", 1)))
    around = [rim[i, j] for i in range(3) for j in range(3) if (i, j) != (1, 1)]
    seg_all = jnp.concatenate([own] + around, axis=1)
    force = contact(state, seg_all, tile_list, pair_mask, tile_count, STIFFNESS, DAMPING)
    return scatter(swap(force), pack_index, positions.shape[1])


def solution(mesh):
    return jax.shard_map(
        on_device,
        mesh=mesh,
        in_specs=(
            P(None, AXES),
            P(None, AXES),
            P(AXES),
            P(AXES),
            P(AXES, None),
            P(AXES, None),
            P(None, AXES),
            P(AXES, None),
            P(AXES),
        ),
        out_specs=P(None, AXES),
        check_vma=False,
    )
```

```python
import functools
import jax
import jax.numpy as jnp
from jax import lax
from jax.experimental import pallas as pl
from jax.experimental.pallas import tpu as pltpu
from jax.sharding import PartitionSpec as P

F32 = jnp.float32
BF16 = jnp.bfloat16
I32 = jnp.int32
CHUNK = 256
GROUP = 4
LOG2E = 1.4426950408889634


def iota(shape, axis):
    return lax.broadcasted_iota(I32, shape, axis)


def split3(x):
    high = x.astype(BF16)
    rest = x - high.astype(F32)
    middle = rest.astype(BF16)
    low = (rest - middle.astype(F32)).astype(BF16)
    return high, middle, low


def expand_rows(tile):
    rows = tile.shape[0]
    high, middle, low = split3(tile)
    parts = [high.astype(F32), middle.astype(F32), low.astype(F32)]
    stacked = jnp.concatenate(parts, axis=0).astype(BF16)
    spread = (iota((3 * rows, 128), 0) % rows == iota((3 * rows, 128), 1) % 8).astype(F32).astype(BF16)
    return lax.dot_general(stacked, spread, (((0,), (0,)), ((), ())), preferred_element_type=F32)


def merge_groups(rows, shape):
    lane = iota(shape, 1)
    bit = 8
    while len(rows) > 1:
        odd = (lane & bit) != 0
        rows = [jnp.where(odd, rows[2 * i + 1], rows[2 * i]) for i in range(len(rows) // 2)]
        bit *= 2
    return rows[0]


def feature_major(rows):
    lane = iota((8, 128), 1)
    pick = (lane // 8) * 8 + iota((8, 128), 0)
    out = None
    for r in range(8):
        moved = jnp.take_along_axis(rows[r], pick, axis=1)
        out = moved if out is None else jnp.where(lane % 8 == r, moved, out)
    return out


def index_chunks(index_ref, body):
    def turn(i, carry):
        body(i, lambda k: index_ref[0, i * CHUNK + k])
        return carry

    lax.fori_loop(0, index_ref.shape[1] // CHUNK, turn, 0, unroll=2)


def pack_kernel(index_ref, pos_ref, vel_ref, mass_ref, thick_ref, out_ref, rows_ref):
    nodes = pos_ref.shape[1]

    def fill(b, carry):
        at = pl.ds(pl.multiple_of(b * 128, 128), 128)
        tile = jnp.concatenate([pos_ref[:, at], vel_ref[:, at], mass_ref[:, at], thick_ref[:, at]], axis=0)
        rows_ref[at, :] = expand_rows(tile)
        return carry

    lax.fori_loop(0, nodes // 128, fill, 0, unroll=8)
    rows_ref[nodes : nodes + 8, :] = jnp.zeros((8, 128), F32)

    def chunk(c, index):
        for half in range(CHUNK // 128):
            lines = []
            for r in range(8):
                got = [
                    rows_ref[pl.ds(index(half * 128 + k * 8 + r), 8, stride=0), :] for k in range(16)
                ]
                lines.append(merge_groups(got, (8, 128)))
            out_ref[c * (CHUNK // 128) + half] = feature_major(lines)

    index_chunks(index_ref, chunk)


VMEM = pl.BlockSpec(memory_space=pltpu.VMEM)
SMEM = pl.BlockSpec(memory_space=pltpu.SMEM)


def pack(positions, velocities, nodal_mass, thickness, pack_index):
    nodes = positions.shape[1]
    return pl.pallas_call(
        pack_kernel,
        out_shape=jax.ShapeDtypeStruct((pack_index.shape[1] // 128, 8, 128), F32),
        in_specs=[SMEM, VMEM, VMEM, VMEM, VMEM],
        out_specs=VMEM,
        scratch_shapes=[
            pltpu.VMEM((nodes + 8, 128), F32),
        ],
        compiler_params=pltpu.CompilerParams(vmem_limit_bytes=48 << 20),
        name="pack",
    )(pack_index, positions, velocities, nodal_mass.reshape(1, -1), thickness.reshape(1, -1))


def scatter_kernel(index_ref, force_ref, out_ref, rows_ref, ex_a, ex_b):
    nodes = out_ref.shape[1]

    def chunk(c, index):
        for half, ex in enumerate((ex_a, ex_b)):
            ex[...] = expand_rows(force_ref[c * 2 + half])
            for j in range(128):
                rows_ref[pl.ds(index(half * 128 + j), 1), :] = ex[j : j + 1, :]

    index_chunks(index_ref, chunk)

    def collect(b, carry):
        at = pl.multiple_of(b * 128, 128)
        tiles = [rows_ref[pl.ds(at + k * 8, 8), :] for k in range(16)]
        merged = merge_groups(tiles, (8, 128))
        lines = [jnp.broadcast_to(merged[r : r + 1], (8, 128)) for r in range(8)]
        out_ref[:, pl.ds(at, 128)] = feature_major(lines)[0:3]
        return carry

    lax.fori_loop(0, nodes // 128, collect, 0, unroll=4)


def scatter(force, pack_index, nodes):
    return pl.pallas_call(
        scatter_kernel,
        out_shape=jax.ShapeDtypeStruct((3, nodes), F32),
        in_specs=[SMEM, VMEM],
        out_specs=VMEM,
        scratch_shapes=[
            pltpu.VMEM((nodes + 8, 128), F32),
            pltpu.VMEM((128, 128), F32),
            pltpu.VMEM((128, 128), F32),
        ],
        compiler_params=pltpu.CompilerParams(vmem_limit_bytes=48 << 20),
        name="scatter",
    )(pack_index, force)


def features_kernel(conn_ref, state_ref, out_ref):
    lane = iota((8, 128), 1)

    def chunk(c, carry):
        corner = []
        for i in range(4):
            found = jnp.zeros((8, 128), F32)
            for q in range(128):
                slot = conn_ref[i, c * 128 + q]
                tile = state_ref[slot >> 7]
                moved = pltpu.roll(tile, (q - slot) & 127, axis=1)
                found = jnp.where(lane == q, moved, found)
            corner.append(found)
        total = (corner[0] + corner[1] + corner[2] + corner[3]) * 0.25
        centre = total[0:3]
        d1 = corner[2] - corner[0]
        d2 = corner[3] - corner[1]
        w0 = d1[1:2] * d2[2:3] - d1[2:3] * d2[1:2]
        w1 = d1[2:3] * d2[0:1] - d1[0:1] * d2[2:3]
        w2 = d1[0:1] * d2[1:2] - d1[1:2] * d2[0:1]
        scale = jnp.maximum(jnp.sqrt(w0 * w0 + w1 * w1 + w2 * w2), 1.0)
        off = [corner[i][0:3] - centre for i in range(4)]
        square = off[0] * off[0] + off[1] * off[1] + off[2] * off[2] + off[3] * off[3]
        spread = (square[0:1] + square[1:2] + square[2:3]) * 0.25
        at = pl.ds(pl.multiple_of(c * 128, 128), 128)
        out_ref[0:3, at] = centre
        out_ref[3:6, at] = jnp.concatenate([w0 / scale, w1 / scale, w2 / scale], axis=0)
        out_ref[6:9, at] = total[3:6]
        out_ref[9:10, at] = spread
        return carry

    lax.fori_loop(0, out_ref.shape[1] // 128, chunk, 0)


def features(connectivity, state):
    segs = connectivity.shape[0]
    return pl.pallas_call(
        features_kernel,
        out_shape=jax.ShapeDtypeStruct((10, segs), F32),
        in_specs=[SMEM, VMEM],
        out_specs=VMEM,
        compiler_params=pltpu.CompilerParams(vmem_limit_bytes=16 << 20),
        name="features",
    )(connectivity.T, state)


def contact_kernel(tiles_ref, count_ref, state_ref, seg_ref, mask_ref, out_ref, coef_ref, normal_ref, keep_a, keep_b, *, stiffness, damping):
    blocks = state_ref.shape[0]
    seg_blocks = seg_ref.shape[1] // 256
    out_ref[...] = jnp.zeros_like(out_ref)

    def prepare(s, carry):
        f = seg_ref[:, pl.ds(pl.multiple_of(s * 256, 256), 256)]
        n = f[3:6]
        rate = LOG2E / (f[9:10] + 0.25)
        one = jnp.ones((1, 256), F32)
        zero = jnp.zeros((3, 256), F32)
        dot = lambda a, b: jnp.sum(a * b, axis=0, keepdims=True)
        sides = (
            [-n, dot(f[0:3], n), one],
            [2.0 * rate * f[0:3], -rate * dot(f[0:3], f[0:3]), -rate],
            [-damping * n, damping * dot(f[6:9], n), stiffness * one],
        )
        for i, rows in enumerate(sides):
            high, middle, low = split3(jnp.concatenate(rows + [zero], axis=0))
            coef_ref[s, i] = pack6([high, high, high, middle, middle, low]).T
        high, middle, _ = split3(n)
        normal_ref[s] = jnp.concatenate([high.astype(F32), middle.astype(F32), zero[0:2]], axis=0)
        return carry

    lax.fori_loop(0, seg_blocks, prepare, 0)
    total = count_ref[0]
    row = iota((8, 128), 0)

    def first(t, keep_ref, slot):
        block = tiles_ref[0, t]
        node = state_ref[block]
        sq = jnp.sum(jnp.where(row < 3, node * node, 0.0), axis=0, keepdims=True)
        one = jnp.ones((1, 128), F32)
        zero = jnp.zeros((3, 128), F32)
        sides = (
            [node[0:3], one, node[7:8]],
            [node[0:3], one, sq],
            [node[3:6], one, node[6:7]],
        )
        left = []
        for rows in sides:
            high, middle, low = split3(jnp.concatenate(rows + [zero], axis=0))
            left.append(pack6([high, middle, low, high, middle, high]))
        for half in range(2):
            s = tiles_ref[1, t + half * blocks]
            term = [jnp.dot(coef_ref[s, i], left[i], preferred_element_type=F32) for i in range(3)]
            size = jnp.maximum(term[0], 0.0) * jnp.exp2(term[1]) * term[2]
            top = size.astype(BF16)
            keep_ref[2 * slot + half, 0] = top
            keep_ref[2 * slot + half, 1] = (size - top.astype(F32)).astype(BF16)

    def second(t, keep_ref, slot, on):
        force = jnp.zeros((8, 128), F32)
        for half in range(2):
            e = t + half * blocks
            live = jnp.where(e < total, on, 0.0)
            mask = mask_ref[pl.ds(e, 1), :].astype(F32) * live
            weights = (normal_ref[tiles_ref[1, e]] * mask).astype(BF16)
            for part in range(2):
                force += jnp.dot(weights, keep_ref[2 * slot + half, part], preferred_element_type=F32)
        out_ref[tiles_ref[0, t], 0:3] = force[0:3] + force[3:6]

    keep_b[...] = jnp.zeros_like(keep_b)

    def turn(i, carry):
        t = i * (2 * GROUP)
        before = jnp.maximum(t - GROUP, 0)
        on = jnp.where(i > 0, 1.0, 0.0)
        for k in range(GROUP):
            first(t + k, keep_a, k)
            second(before + k, keep_b, k, on)
        for k in range(GROUP):
            first(t + GROUP + k, keep_b, k)
            second(t + k, keep_a, k, 1.0)
        return carry

    turns = (jnp.minimum(total, blocks) + 2 * GROUP - 1) // (2 * GROUP)
    lax.fori_loop(0, turns, turn, 0)
    for k in range(GROUP):
        second(turns * 2 * GROUP - GROUP + k, keep_b, k, 1.0)


def pack6(parts):
    return jnp.concatenate([p.astype(F32) for p in parts], axis=0).astype(BF16)


def contact(state, seg_all, tile_list, pair_mask, tile_count, stiffness, damping):
    blocks = state.shape[0]
    seg_blocks = seg_all.shape[1] // 256
    return pl.pallas_call(
        functools.partial(contact_kernel, stiffness=stiffness, damping=damping),
        out_shape=jax.ShapeDtypeStruct((blocks, 4, 128), F32),
        in_specs=[SMEM, SMEM, VMEM, VMEM, VMEM],
        out_specs=VMEM,
        scratch_shapes=[
            pltpu.VMEM((seg_blocks, 3, 256, 48), BF16),
            pltpu.VMEM((seg_blocks, 8, 256), F32),
            pltpu.VMEM((2 * GROUP, 2, 256, 128), BF16),
            pltpu.VMEM((2 * GROUP, 2, 256, 128), BF16),
        ],
        compiler_params=pltpu.CompilerParams(vmem_limit_bytes=32 << 20),
        name="contact",
    )(tile_list, tile_count, state, seg_all, pair_mask)

STIFFNESS = 1.0
DAMPING = 0.3
AXES = ("wide", "narrow")


def swap(blocks):
    return lax.all_to_all(blocks, AXES, split_axis=0, concat_axis=0, tiled=True)


def padded(cells, sides):
    for axis, dim in sides:
        ends = lax.axis_size(axis) - 1
        head = lax.slice_in_dim(cells, 0, 1, axis=dim)
        tail = lax.slice_in_dim(cells, cells.shape[dim] - 1, cells.shape[dim], axis=dim)
        before = lax.ppermute(tail, axis, [(i, i + 1) for i in range(ends)])
        after = lax.ppermute(head, axis, [(i + 1, i) for i in range(ends)])
        cells = jnp.concatenate([before, cells, after], axis=dim)
    return cells


def on_device(positions, velocities, nodal_mass, thickness, pack_index, connectivity, tile_list, pair_mask, tile_count):
    state = swap(pack(positions, velocities, nodal_mass, thickness, pack_index))
    own = features(connectivity, state)
    ghosts = connectivity.shape[0] // 4
    rim = padded(own[None, None, :, :ghosts], (("wide", 0), ("narrow", 1)))
    around = [rim[i, j] for i in range(3) for j in range(3) if (i, j) != (1, 1)]
    seg_all = jnp.concatenate([own] + around, axis=1)
    force = contact(state, seg_all, tile_list, pair_mask, tile_count, STIFFNESS, DAMPING)
    return scatter(swap(force), pack_index, positions.shape[1])


def solution(mesh):
    return jax.shard_map(
        on_device,
        mesh=mesh,
        in_specs=(
            P(None, AXES),
            P(None, AXES),
            P(AXES),
            P(AXES),
            P(AXES, None),
            P(AXES, None),
            P(None, AXES),
            P(AXES, None),
            P(AXES),
        ),
        out_specs=P(None, AXES),
        check_vma=False,
    )
```

```python
import functools
import jax
import jax.numpy as jnp
from jax import lax
from jax.experimental import pallas as pl
from jax.experimental.pallas import tpu as pltpu
from jax.sharding import PartitionSpec as P

F32 = jnp.float32
BF16 = jnp.bfloat16
I32 = jnp.int32
CHUNK = 512
UNR = 1
GROUP = 4
LOG2E = 1.4426950408889634


def iota(shape, axis):
    return lax.broadcasted_iota(I32, shape, axis)


def split3(x):
    high = x.astype(BF16)
    rest = x - high.astype(F32)
    middle = rest.astype(BF16)
    low = (rest - middle.astype(F32)).astype(BF16)
    return high, middle, low


def expand_rows(tile):
    rows = tile.shape[0]
    high, middle, low = split3(tile)
    parts = [high.astype(F32), middle.astype(F32), low.astype(F32)]
    stacked = jnp.concatenate(parts, axis=0).astype(BF16)
    spread = (iota((3 * rows, 128), 0) % rows == iota((3 * rows, 128), 1) % 8).astype(F32).astype(BF16)
    return lax.dot_general(stacked, spread, (((0,), (0,)), ((), ())), preferred_element_type=F32)


def merge_groups(rows, shape):
    lane = iota(shape, 1)
    bit = 8
    while len(rows) > 1:
        odd = (lane & bit) != 0
        rows = [jnp.where(odd, rows[2 * i + 1], rows[2 * i]) for i in range(len(rows) // 2)]
        bit *= 2
    return rows[0]


def feature_major(rows):
    lane = iota((8, 128), 1)
    pick = (lane // 8) * 8 + iota((8, 128), 0)
    out = None
    for r in range(8):
        moved = jnp.take_along_axis(rows[r], pick, axis=1)
        out = moved if out is None else jnp.where(lane % 8 == r, moved, out)
    return out


def index_chunks(index_ref, body):
    def turn(i, carry):
        body(i, lambda k: index_ref.at[k][i])
        return carry

    lax.fori_loop(0, index_ref.shape[1], turn, 0, unroll=UNR)


def merge_lanes(tiles):
    lane = iota((8, 128), 1)
    bit = 1
    while len(tiles) > 1:
        odd = (lane & bit) != 0
        tiles = [jnp.where(odd, tiles[2 * i + 1], tiles[2 * i]) for i in range(len(tiles) // 2)]
        bit *= 2
    return tiles[0]


def pick_lanes(row_of, lanes, table_ref):
    spread = jnp.broadcast_to(lanes, (8, 128))
    return merge_lanes([jnp.take_along_axis(table_ref[row_of(j)], spread, axis=1) for j in range(128)])


def pack_kernel(index_ref, pos_ref, vel_ref, mass_ref, thick_ref, out_ref, rows_ref):
    nodes = pos_ref.shape[1]

    def fill(b, carry):
        at = pl.ds(pl.multiple_of(b * 128, 128), 128)
        tile = jnp.concatenate([pos_ref[:, at], vel_ref[:, at], mass_ref[:, at], thick_ref[:, at]], axis=0)
        rows_ref[at, :] = expand_rows(tile)
        return carry

    lax.fori_loop(0, nodes // 128, fill, 0, unroll=8)
    rows_ref[nodes : nodes + 8, :] = jnp.zeros((8, 128), F32)

    def chunk(c, index):
        for half in range(CHUNK // 128):
            lines = []
            for r in range(8):
                got = [
                    rows_ref[pl.ds(index(half * 128 + k * 8 + r), 8, stride=0), :] for k in range(16)
                ]
                lines.append(merge_groups(got, (8, 128)))
            out_ref[c * (CHUNK // 128) + half] = feature_major(lines)

    index_chunks(index_ref, chunk)


VMEM = pl.BlockSpec(memory_space=pltpu.VMEM)
SMEM = pl.BlockSpec(memory_space=pltpu.SMEM)


def columns(pack_index):
    return pack_index.reshape(-1, CHUNK).T


def pack(positions, velocities, nodal_mass, thickness, pack_index):
    nodes = positions.shape[1]
    return pl.pallas_call(
        pack_kernel,
        out_shape=jax.ShapeDtypeStruct((pack_index.shape[1] // 128, 8, 128), F32),
        in_specs=[SMEM, VMEM, VMEM, VMEM, VMEM],
        out_specs=VMEM,
        scratch_shapes=[
            pltpu.VMEM((nodes + 8, 128), F32),
        ],
        compiler_params=pltpu.CompilerParams(vmem_limit_bytes=48 << 20),
        name="pack",
    )(columns(pack_index), positions, velocities, nodal_mass.reshape(1, -1), thickness.reshape(1, -1))


def scatter_kernel(index_ref, force_ref, out_ref, rows_ref, ex_a, ex_b):
    nodes = out_ref.shape[1]
    chunks = index_ref.shape[1]
    tiles = CHUNK // 128

    def spread(c, ex_ref):
        for part in range(tiles):
            ex_ref[part * 128 : part * 128 + 128] = expand_rows(force_ref[c * tiles + part])

    def place(c, ex_ref):
        for j in range(CHUNK):
            rows_ref[pl.ds(index_ref.at[j][c], 1), :] = ex_ref[j : j + 1, :]

    spread(0, ex_a)

    def turn(i, carry):
        spread(2 * i + 1, ex_b)
        place(2 * i, ex_a)
        spread(jnp.minimum(2 * i + 2, chunks - 1), ex_a)
        place(2 * i + 1, ex_b)
        return carry

    lax.fori_loop(0, chunks // 2, turn, 0)

    def collect(b, carry):
        at = pl.multiple_of(b * 128, 128)
        tiles = [rows_ref[pl.ds(at + k * 8, 8), :] for k in range(16)]
        merged = merge_groups(tiles, (8, 128))
        lines = [jnp.broadcast_to(merged[r : r + 1], (8, 128)) for r in range(8)]
        out_ref[:, pl.ds(at, 128)] = feature_major(lines)[0:3]
        return carry

    lax.fori_loop(0, nodes // 128, collect, 0, unroll=8)


def scatter(force, pack_index, nodes):
    return pl.pallas_call(
        scatter_kernel,
        out_shape=jax.ShapeDtypeStruct((3, nodes), F32),
        in_specs=[SMEM, VMEM],
        out_specs=VMEM,
        scratch_shapes=[
            pltpu.VMEM((nodes + 8, 128), F32),
            pltpu.VMEM((CHUNK, 128), F32),
            pltpu.VMEM((CHUNK, 128), F32),
        ],
        compiler_params=pltpu.CompilerParams(vmem_limit_bytes=48 << 20),
        name="scatter",
    )(columns(pack_index), force)


def merge_lanes(tiles):
    lane = iota((8, 128), 1)
    bit = 1
    while len(tiles) > 1:
        odd = (lane & bit) != 0
        tiles = [jnp.where(odd, tiles[2 * i + 1], tiles[2 * i]) for i in range(len(tiles) // 2)]
        bit *= 2
    return tiles[0]


def pick_lanes(row_of, lanes, table_ref):
    spread = jnp.broadcast_to(lanes, (8, 128))
    return merge_lanes([jnp.take_along_axis(table_ref[row_of(j)], spread, axis=1) for j in range(128)])


def features_kernel(row_ref, lane_ref, state_ref, out_ref):
    def chunk(c, carry):
        corner = []
        for i in range(4):
            row_of = lambda q: row_ref.at[i * 128 + q][c]
            corner.append(pick_lanes(row_of, lane_ref[pl.ds(i, 1), pl.ds(pl.multiple_of(c * 128, 128), 128)], state_ref))
        total = (corner[0] + corner[1] + corner[2] + corner[3]) * 0.25
        centre = total[0:3]
        d1 = corner[2] - corner[0]
        d2 = corner[3] - corner[1]
        w0 = d1[1:2] * d2[2:3] - d1[2:3] * d2[1:2]
        w1 = d1[2:3] * d2[0:1] - d1[0:1] * d2[2:3]
        w2 = d1[0:1] * d2[1:2] - d1[1:2] * d2[0:1]
        scale = jnp.maximum(jnp.sqrt(w0 * w0 + w1 * w1 + w2 * w2), 1.0)
        off = [corner[i][0:3] - centre for i in range(4)]
        square = off[0] * off[0] + off[1] * off[1] + off[2] * off[2] + off[3] * off[3]
        spread = (square[0:1] + square[1:2] + square[2:3]) * 0.25
        at = pl.ds(pl.multiple_of(c * 128, 128), 128)
        out_ref[0:3, at] = centre
        out_ref[3:6, at] = jnp.concatenate([w0 / scale, w1 / scale, w2 / scale], axis=0)
        out_ref[6:9, at] = total[3:6]
        out_ref[9:10, at] = spread
        return carry

    lax.fori_loop(0, out_ref.shape[1] // 128, chunk, 0)


def corner_rows(connectivity):
    rows = (connectivity >> 7).T.reshape(4, -1, 128)
    rows = jnp.transpose(rows, (0, 2, 1)).reshape(512, -1)
    return jnp.pad(rows, ((0, 0), (0, 128 - rows.shape[1])))


def features(connectivity, state):
    segs = connectivity.shape[0]
    return pl.pallas_call(
        features_kernel,
        out_shape=jax.ShapeDtypeStruct((10, segs), F32),
        in_specs=[SMEM, VMEM, VMEM],
        out_specs=VMEM,
        compiler_params=pltpu.CompilerParams(vmem_limit_bytes=16 << 20),
        name="features",
    )(corner_rows(connectivity), (connectivity & 127).T, state)


def contact_kernel(tiles_ref, count_ref, state_ref, seg_ref, mask_ref, out_ref, coef_ref, normal_ref, keep_a, keep_b, *, stiffness, damping):
    blocks = state_ref.shape[0]
    seg_blocks = seg_ref.shape[1] // 256
    out_ref[...] = jnp.zeros_like(out_ref)

    def prepare(s, carry):
        f = seg_ref[:, pl.ds(pl.multiple_of(s * 256, 256), 256)]
        n = f[3:6]
        rate = LOG2E / (f[9:10] + 0.25)
        one = jnp.ones((1, 256), F32)
        zero = jnp.zeros((3, 256), F32)
        dot = lambda a, b: jnp.sum(a * b, axis=0, keepdims=True)
        sides = (
            [-n, dot(f[0:3], n), one],
            [2.0 * rate * f[0:3], -rate * dot(f[0:3], f[0:3]), -rate],
            [-damping * n, damping * dot(f[6:9], n), stiffness * one],
        )
        for i, rows in enumerate(sides):
            high, middle, low = split3(jnp.concatenate(rows + [zero], axis=0))
            coef_ref[s, i] = pack6([high, high, high, middle, middle, low]).T
        high, middle, _ = split3(n)
        normal_ref[s] = jnp.concatenate([high.astype(F32), middle.astype(F32), zero[0:2]], axis=0)
        return carry

    lax.fori_loop(0, seg_blocks, prepare, 0)
    total = count_ref[0]
    row = iota((8, 128), 0)

    def first(t, keep_ref, slot):
        block = tiles_ref[0, t]
        node = state_ref[block]
        sq = jnp.sum(jnp.where(row < 3, node * node, 0.0), axis=0, keepdims=True)
        one = jnp.ones((1, 128), F32)
        zero = jnp.zeros((3, 128), F32)
        sides = (
            [node[0:3], one, node[7:8]],
            [node[0:3], one, sq],
            [node[3:6], one, node[6:7]],
        )
        left = []
        for rows in sides:
            high, middle, low = split3(jnp.concatenate(rows + [zero], axis=0))
            left.append(pack6([high, middle, low, high, middle, high]))
        for half in range(2):
            s = tiles_ref[1, t + half * blocks]
            term = [jnp.dot(coef_ref[s, i], left[i], preferred_element_type=F32) for i in range(3)]
            size = jnp.maximum(term[0], 0.0) * jnp.exp2(term[1]) * term[2]
            top = size.astype(BF16)
            keep_ref[2 * slot + half, 0] = top
            keep_ref[2 * slot + half, 1] = (size - top.astype(F32)).astype(BF16)

    def second(t, keep_ref, slot, on):
        force = jnp.zeros((8, 128), F32)
        for half in range(2):
            e = t + half * blocks
            live = jnp.where(e < total, on, 0.0)
            mask = mask_ref[pl.ds(e, 1), :].astype(F32) * live
            weights = (normal_ref[tiles_ref[1, e]] * mask).astype(BF16)
            for part in range(2):
                force += jnp.dot(weights, keep_ref[2 * slot + half, part], preferred_element_type=F32)
        out_ref[tiles_ref[0, t], 0:3] = force[0:3] + force[3:6]

    keep_b[...] = jnp.zeros_like(keep_b)

    def turn(i, carry):
        t = i * (2 * GROUP)
        before = jnp.maximum(t - GROUP, 0)
        on = jnp.where(i > 0, 1.0, 0.0)
        for k in range(GROUP):
            first(t + k, keep_a, k)
            second(before + k, keep_b, k, on)
        for k in range(GROUP):
            first(t + GROUP + k, keep_b, k)
            second(t + k, keep_a, k, 1.0)
        return carry

    turns = (jnp.minimum(total, blocks) + 2 * GROUP - 1) // (2 * GROUP)
    lax.fori_loop(0, turns, turn, 0)
    for k in range(GROUP):
        second(turns * 2 * GROUP - GROUP + k, keep_b, k, 1.0)


def pack6(parts):
    return jnp.concatenate([p.astype(F32) for p in parts], axis=0).astype(BF16)


def contact(state, seg_all, tile_list, pair_mask, tile_count, stiffness, damping):
    blocks = state.shape[0]
    seg_blocks = seg_all.shape[1] // 256
    return pl.pallas_call(
        functools.partial(contact_kernel, stiffness=stiffness, damping=damping),
        out_shape=jax.ShapeDtypeStruct((blocks, 4, 128), F32),
        in_specs=[SMEM, SMEM, VMEM, VMEM, VMEM],
        out_specs=VMEM,
        scratch_shapes=[
            pltpu.VMEM((seg_blocks, 3, 256, 48), BF16),
            pltpu.VMEM((seg_blocks, 8, 256), F32),
            pltpu.VMEM((2 * GROUP, 2, 256, 128), BF16),
            pltpu.VMEM((2 * GROUP, 2, 256, 128), BF16),
        ],
        compiler_params=pltpu.CompilerParams(vmem_limit_bytes=32 << 20),
        name="contact",
    )(tile_list, tile_count, state, seg_all, pair_mask)

STIFFNESS = 1.0
DAMPING = 0.3
AXES = ("wide", "narrow")


def swap(blocks):
    return lax.all_to_all(blocks, AXES, split_axis=0, concat_axis=0, tiled=True)


def padded(cells, sides):
    for axis, dim in sides:
        ends = lax.axis_size(axis) - 1
        head = lax.slice_in_dim(cells, 0, 1, axis=dim)
        tail = lax.slice_in_dim(cells, cells.shape[dim] - 1, cells.shape[dim], axis=dim)
        before = lax.ppermute(tail, axis, [(i, i + 1) for i in range(ends)])
        after = lax.ppermute(head, axis, [(i + 1, i) for i in range(ends)])
        cells = jnp.concatenate([before, cells, after], axis=dim)
    return cells


def on_device(positions, velocities, nodal_mass, thickness, pack_index, connectivity, tile_list, pair_mask, tile_count):
    state = swap(pack(positions, velocities, nodal_mass, thickness, pack_index))
    own = features(connectivity, state)
    ghosts = connectivity.shape[0] // 4
    rim = padded(own[None, None, :, :ghosts], (("wide", 0), ("narrow", 1)))
    around = [rim[i, j] for i in range(3) for j in range(3) if (i, j) != (1, 1)]
    seg_all = jnp.concatenate([own] + around, axis=1)
    force = contact(state, seg_all, tile_list, pair_mask, tile_count, STIFFNESS, DAMPING)
    return scatter(swap(force), pack_index, positions.shape[1])


def solution(mesh):
    return jax.shard_map(
        on_device,
        mesh=mesh,
        in_specs=(
            P(None, AXES),
            P(None, AXES),
            P(AXES),
            P(AXES),
            P(AXES, None),
            P(AXES, None),
            P(None, AXES),
            P(AXES, None),
            P(AXES),
        ),
        out_specs=P(None, AXES),
        check_vma=False,
    )
```

```python
import functools
import jax
import jax.numpy as jnp
from jax import lax
from jax.experimental import pallas as pl
from jax.experimental.pallas import tpu as pltpu
from jax.sharding import PartitionSpec as P

F32 = jnp.float32
BF16 = jnp.bfloat16
I32 = jnp.int32
CHUNK = 512
UNR = 1
GROUP = 4
LOG2E = 1.4426950408889634


def iota(shape, axis):
    return lax.broadcasted_iota(I32, shape, axis)


def split3(x):
    high = x.astype(BF16)
    rest = x - high.astype(F32)
    middle = rest.astype(BF16)
    low = (rest - middle.astype(F32)).astype(BF16)
    return high, middle, low


def expand_rows(tile):
    rows = tile.shape[0]
    high, middle, low = split3(tile)
    parts = [high.astype(F32), middle.astype(F32), low.astype(F32)]
    stacked = jnp.concatenate(parts, axis=0).astype(BF16)
    spread = (iota((3 * rows, 128), 0) % rows == iota((3 * rows, 128), 1) % 8).astype(F32).astype(BF16)
    return lax.dot_general(stacked, spread, (((0,), (0,)), ((), ())), preferred_element_type=F32)


def merge_groups(rows, shape):
    lane = iota(shape, 1)
    bit = 8
    while len(rows) > 1:
        odd = (lane & bit) != 0
        rows = [jnp.where(odd, rows[2 * i + 1], rows[2 * i]) for i in range(len(rows) // 2)]
        bit *= 2
    return rows[0]


def feature_major(rows):
    lane = iota((8, 128), 1)
    pick = (lane // 8) * 8 + iota((8, 128), 0)
    out = None
    for r in range(8):
        moved = jnp.take_along_axis(rows[r], pick, axis=1)
        out = moved if out is None else jnp.where(lane % 8 == r, moved, out)
    return out


def index_chunks(index_ref, body):
    def turn(i, carry):
        body(i, lambda k: index_ref.at[k][i])
        return carry

    lax.fori_loop(0, index_ref.shape[1], turn, 0, unroll=UNR)


def merge_lanes(tiles):
    lane = iota((8, 128), 1)
    bit = 1
    while len(tiles) > 1:
        odd = (lane & bit) != 0
        tiles = [jnp.where(odd, tiles[2 * i + 1], tiles[2 * i]) for i in range(len(tiles) // 2)]
        bit *= 2
    return tiles[0]


def pick_lanes(row_of, lanes, table_ref):
    spread = jnp.broadcast_to(lanes, (8, 128))
    return merge_lanes([jnp.take_along_axis(table_ref[row_of(j)], spread, axis=1) for j in range(128)])


WIDE, NARROW = "wide", "narrow"


def my_place():
    wide, narrow = lax.axis_index(WIDE), lax.axis_index(NARROW)
    return wide // 4, wide % 4, narrow // 2, narrow % 2


def my_number():
    return lax.axis_index(WIDE) * 8 + lax.axis_index(NARROW)


def peer(i):
    z, x, y, core = my_place()
    dz = i % 4
    dx = (i // 4 + i) % 4
    dy = (i // 16 + i // 4 + i) % 4
    dc = (i // 64) % 2
    return ((z + dz) % 4) * 4 + (x + dx) % 4, ((y + dy) % 4) * 2 + (core + dc) % 2


def greet(barrier, peers):
    def one(i, carry):
        pl.semaphore_signal(barrier, inc=1, device_id=peer(i), device_id_type=pl.DeviceIdType.MESH)
        return carry

    lax.fori_loop(1, peers, one, 0)


def block_copy(source_ref, target_ref, send_sem, recv_sem, i):
    wide, narrow = peer(i)
    number = wide * 8 + narrow
    return pltpu.make_async_remote_copy(
        src_ref=source_ref.at[number],
        dst_ref=target_ref.at[my_number()],
        send_sem=send_sem.at[number],
        recv_sem=recv_sem.at[my_number()],
        device_id=(wide, narrow),
        device_id_type=pl.DeviceIdType.MESH,
    )


def wait_blocks(source_ref, target_ref, send_sem, recv_sem, peers):
    def one(i, carry):
        wide, narrow = peer(i)
        number = wide * 8 + narrow
        copy = pltpu.make_async_remote_copy(
            src_ref=source_ref.at[number],
            dst_ref=target_ref.at[number],
            send_sem=send_sem.at[number],
            recv_sem=recv_sem.at[number],
            device_id=(wide, narrow),
            device_id_type=pl.DeviceIdType.MESH,
        )
        copy.wait_send()
        copy.wait_recv()
        return carry

    lax.fori_loop(1, peers, one, 0)


def pack_kernel(
    index_ref, pos_ref, vel_ref, mass_ref, thick_ref, out_ref, rows_ref, stage_ref, send_sem, recv_sem, own_sem
):
    nodes = pos_ref.shape[1]
    peers = out_ref.shape[0]
    barrier = pltpu.get_barrier_semaphore()
    greet(barrier, peers)

    def fill(b, carry):
        at = pl.ds(pl.multiple_of(b * 128, 128), 128)
        tile = jnp.concatenate([pos_ref[:, at], vel_ref[:, at], mass_ref[:, at], thick_ref[:, at]], axis=0)
        rows_ref[at, :] = expand_rows(tile)
        return carry

    lax.fori_loop(0, nodes // 128, fill, 0, unroll=8)
    rows_ref[nodes : nodes + 8, :] = jnp.zeros((8, 128), F32)
    pl.semaphore_wait(barrier, peers - 1)

    def turn(i, carry):
        wide, narrow = peer((i + 1) % peers)
        number = wide * 8 + narrow
        for part in range(CHUNK // 128):
            lines = []
            for r in range(8):
                got = [rows_ref[pl.ds(index_ref.at[part * 128 + k * 8 + r][number], 1), :] for k in range(16)]
                lines.append(jnp.broadcast_to(merge_groups(got, (1, 128)), (8, 128)))
            stage_ref[number, part] = feature_major(lines)

        @pl.when(i > 0)
        def _():
            block_copy(stage_ref, out_ref, send_sem, recv_sem, i).start()

        return carry

    lax.fori_loop(0, peers, turn, 0)
    me = my_number()
    own = pltpu.make_async_copy(stage_ref.at[me], out_ref.at[me], own_sem)
    own.start()
    wait_blocks(stage_ref, out_ref, send_sem, recv_sem, peers)
    own.wait()


VMEM = pl.BlockSpec(memory_space=pltpu.VMEM)
SMEM = pl.BlockSpec(memory_space=pltpu.SMEM)


def columns(pack_index):
    return pack_index.reshape(-1, CHUNK).T


def pack(positions, velocities, nodal_mass, thickness, pack_index):
    nodes = positions.shape[1]
    blocks = (pack_index.shape[1] // CHUNK, CHUNK // 128, 8, 128)
    return pl.pallas_call(
        pack_kernel,
        out_shape=jax.ShapeDtypeStruct(blocks, F32),
        in_specs=[SMEM, VMEM, VMEM, VMEM, VMEM],
        out_specs=VMEM,
        scratch_shapes=[
            pltpu.VMEM((nodes + 8, 128), F32),
            pltpu.VMEM(blocks, F32),
            pltpu.SemaphoreType.DMA((blocks[0],)),
            pltpu.SemaphoreType.DMA((blocks[0],)),
            pltpu.SemaphoreType.DMA,
        ],
        compiler_params=pltpu.CompilerParams(vmem_limit_bytes=48 << 20, collective_id=0, has_side_effects=True),
        name="pack",
    )(columns(pack_index), positions, velocities, nodal_mass.reshape(1, -1), thickness.reshape(1, -1))


def scatter_kernel(index_ref, force_ref, out_ref, rows_ref, ex_a, ex_b):
    nodes = out_ref.shape[1]
    chunks = index_ref.shape[1]
    tiles = CHUNK // 128

    def spread(c, ex_ref):
        for part in range(tiles):
            ex_ref[part * 128 : part * 128 + 128] = expand_rows(force_ref[c * tiles + part])

    def place(c, ex_ref):
        for j in range(CHUNK):
            rows_ref[pl.ds(index_ref.at[j][c], 1), :] = ex_ref[j : j + 1, :]

    spread(0, ex_a)

    def turn(i, carry):
        spread(2 * i + 1, ex_b)
        place(2 * i, ex_a)
        spread(jnp.minimum(2 * i + 2, chunks - 1), ex_a)
        place(2 * i + 1, ex_b)
        return carry

    lax.fori_loop(0, chunks // 2, turn, 0)

    def collect(b, carry):
        at = pl.multiple_of(b * 128, 128)
        tiles = [rows_ref[pl.ds(at + k * 8, 8), :] for k in range(16)]
        merged = merge_groups(tiles, (8, 128))
        lines = [jnp.broadcast_to(merged[r : r + 1], (8, 128)) for r in range(8)]
        out_ref[:, pl.ds(at, 128)] = feature_major(lines)[0:3]
        return carry

    lax.fori_loop(0, nodes // 128, collect, 0, unroll=8)


def scatter(force, pack_index, nodes):
    return pl.pallas_call(
        scatter_kernel,
        out_shape=jax.ShapeDtypeStruct((3, nodes), F32),
        in_specs=[SMEM, VMEM],
        out_specs=VMEM,
        scratch_shapes=[
            pltpu.VMEM((nodes + 8, 128), F32),
            pltpu.VMEM((CHUNK, 128), F32),
            pltpu.VMEM((CHUNK, 128), F32),
        ],
        compiler_params=pltpu.CompilerParams(vmem_limit_bytes=48 << 20),
        name="scatter",
    )(columns(pack_index), force)


def merge_lanes(tiles):
    lane = iota((8, 128), 1)
    bit = 1
    while len(tiles) > 1:
        odd = (lane & bit) != 0
        tiles = [jnp.where(odd, tiles[2 * i + 1], tiles[2 * i]) for i in range(len(tiles) // 2)]
        bit *= 2
    return tiles[0]


def pick_lanes(row_of, lanes, table_ref):
    spread = jnp.broadcast_to(lanes, (8, 128))
    return merge_lanes([jnp.take_along_axis(table_ref[row_of(j)], spread, axis=1) for j in range(128)])


def features_kernel(row_ref, lane_ref, state_ref, out_ref):
    def chunk(c, carry):
        corner = []
        for i in range(4):
            row_of = lambda q: row_ref.at[i * 128 + q][c]
            corner.append(pick_lanes(row_of, lane_ref[pl.ds(i, 1), pl.ds(pl.multiple_of(c * 128, 128), 128)], state_ref))
        total = (corner[0] + corner[1] + corner[2] + corner[3]) * 0.25
        centre = total[0:3]
        d1 = corner[2] - corner[0]
        d2 = corner[3] - corner[1]
        w0 = d1[1:2] * d2[2:3] - d1[2:3] * d2[1:2]
        w1 = d1[2:3] * d2[0:1] - d1[0:1] * d2[2:3]
        w2 = d1[0:1] * d2[1:2] - d1[1:2] * d2[0:1]
        scale = jnp.maximum(jnp.sqrt(w0 * w0 + w1 * w1 + w2 * w2), 1.0)
        off = [corner[i][0:3] - centre for i in range(4)]
        square = off[0] * off[0] + off[1] * off[1] + off[2] * off[2] + off[3] * off[3]
        spread = (square[0:1] + square[1:2] + square[2:3]) * 0.25
        at = pl.ds(pl.multiple_of(c * 128, 128), 128)
        out_ref[0:3, at] = centre
        out_ref[3:6, at] = jnp.concatenate([w0 / scale, w1 / scale, w2 / scale], axis=0)
        out_ref[6:9, at] = total[3:6]
        out_ref[9:10, at] = spread
        return carry

    lax.fori_loop(0, out_ref.shape[1] // 128, chunk, 0)


def corner_rows(connectivity):
    rows = (connectivity >> 7).T.reshape(4, -1, 128)
    rows = jnp.transpose(rows, (0, 2, 1)).reshape(512, -1)
    return jnp.pad(rows, ((0, 0), (0, 128 - rows.shape[1])))


def features(connectivity, state):
    segs = connectivity.shape[0]
    return pl.pallas_call(
        features_kernel,
        out_shape=jax.ShapeDtypeStruct((10, segs), F32),
        in_specs=[SMEM, VMEM, VMEM],
        out_specs=VMEM,
        compiler_params=pltpu.CompilerParams(vmem_limit_bytes=16 << 20),
        name="features",
    )(corner_rows(connectivity), (connectivity & 127).T, state)


def contact_kernel(tiles_ref, count_ref, state_ref, seg_ref, mask_ref, out_ref, coef_ref, normal_ref, keep_a, keep_b, *, stiffness, damping):
    blocks = state_ref.shape[0]
    seg_blocks = seg_ref.shape[1] // 256
    out_ref[...] = jnp.zeros_like(out_ref)

    def prepare(s, carry):
        f = seg_ref[:, pl.ds(pl.multiple_of(s * 256, 256), 256)]
        n = f[3:6]
        rate = LOG2E / (f[9:10] + 0.25)
        one = jnp.ones((1, 256), F32)
        zero = jnp.zeros((3, 256), F32)
        dot = lambda a, b: jnp.sum(a * b, axis=0, keepdims=True)
        sides = (
            [-n, dot(f[0:3], n), one],
            [2.0 * rate * f[0:3], -rate * dot(f[0:3], f[0:3]), -rate],
            [-damping * n, damping * dot(f[6:9], n), stiffness * one],
        )
        for i, rows in enumerate(sides):
            high, middle, low = split3(jnp.concatenate(rows + [zero], axis=0))
            coef_ref[s, i] = pack6([high, high, high, middle, middle, low]).T
        high, middle, _ = split3(n)
        normal_ref[s] = jnp.concatenate([high.astype(F32), middle.astype(F32), zero[0:2]], axis=0)
        return carry

    lax.fori_loop(0, seg_blocks, prepare, 0)
    total = count_ref[0]
    row = iota((8, 128), 0)

    def first(t, keep_ref, slot):
        block = tiles_ref[0, t]
        node = state_ref[block]
        sq = jnp.sum(jnp.where(row < 3, node * node, 0.0), axis=0, keepdims=True)
        one = jnp.ones((1, 128), F32)
        zero = jnp.zeros((3, 128), F32)
        sides = (
            [node[0:3], one, node[7:8]],
            [node[0:3], one, sq],
            [node[3:6], one, node[6:7]],
        )
        left = []
        for rows in sides:
            high, middle, low = split3(jnp.concatenate(rows + [zero], axis=0))
            left.append(pack6([high, middle, low, high, middle, high]))
        for half in range(2):
            s = tiles_ref[1, t + half * blocks]
            term = [jnp.dot(coef_ref[s, i], left[i], preferred_element_type=F32) for i in range(3)]
            size = jnp.maximum(term[0], 0.0) * jnp.exp2(term[1]) * term[2]
            top = size.astype(BF16)
            keep_ref[2 * slot + half, 0] = top
            keep_ref[2 * slot + half, 1] = (size - top.astype(F32)).astype(BF16)

    def second(t, keep_ref, slot, on):
        force = jnp.zeros((8, 128), F32)
        for half in range(2):
            e = t + half * blocks
            live = jnp.where(e < total, on, 0.0)
            mask = mask_ref[pl.ds(e, 1), :].astype(F32) * live
            weights = (normal_ref[tiles_ref[1, e]] * mask).astype(BF16)
            for part in range(2):
                force += jnp.dot(weights, keep_ref[2 * slot + half, part], preferred_element_type=F32)
        out_ref[tiles_ref[0, t], 0:3] = force[0:3] + force[3:6]

    keep_b[...] = jnp.zeros_like(keep_b)

    def turn(i, carry):
        t = i * (2 * GROUP)
        before = jnp.maximum(t - GROUP, 0)
        on = jnp.where(i > 0, 1.0, 0.0)
        for k in range(GROUP):
            first(t + k, keep_a, k)
            second(before + k, keep_b, k, on)
        for k in range(GROUP):
            first(t + GROUP + k, keep_b, k)
            second(t + k, keep_a, k, 1.0)
        return carry

    turns = (jnp.minimum(total, blocks) + 2 * GROUP - 1) // (2 * GROUP)
    lax.fori_loop(0, turns, turn, 0)
    for k in range(GROUP):
        second(turns * 2 * GROUP - GROUP + k, keep_b, k, 1.0)


def pack6(parts):
    return jnp.concatenate([p.astype(F32) for p in parts], axis=0).astype(BF16)


def contact(state, seg_all, tile_list, pair_mask, tile_count, stiffness, damping):
    blocks = state.shape[0]
    seg_blocks = seg_all.shape[1] // 256
    return pl.pallas_call(
        functools.partial(contact_kernel, stiffness=stiffness, damping=damping),
        out_shape=jax.ShapeDtypeStruct((blocks, 4, 128), F32),
        in_specs=[SMEM, SMEM, VMEM, VMEM, VMEM],
        out_specs=VMEM,
        scratch_shapes=[
            pltpu.VMEM((seg_blocks, 3, 256, 48), BF16),
            pltpu.VMEM((seg_blocks, 8, 256), F32),
            pltpu.VMEM((2 * GROUP, 2, 256, 128), BF16),
            pltpu.VMEM((2 * GROUP, 2, 256, 128), BF16),
        ],
        compiler_params=pltpu.CompilerParams(vmem_limit_bytes=32 << 20),
        name="contact",
    )(tile_list, tile_count, state, seg_all, pair_mask)

STIFFNESS = 1.0
DAMPING = 0.3
AXES = ("wide", "narrow")


def swap(blocks):
    return lax.all_to_all(blocks, AXES, split_axis=0, concat_axis=0, tiled=True)


def padded(cells, sides):
    for axis, dim in sides:
        ends = lax.axis_size(axis) - 1
        head = lax.slice_in_dim(cells, 0, 1, axis=dim)
        tail = lax.slice_in_dim(cells, cells.shape[dim] - 1, cells.shape[dim], axis=dim)
        before = lax.ppermute(tail, axis, [(i, i + 1) for i in range(ends)])
        after = lax.ppermute(head, axis, [(i + 1, i) for i in range(ends)])
        cells = jnp.concatenate([before, cells, after], axis=dim)
    return cells


def on_device(positions, velocities, nodal_mass, thickness, pack_index, connectivity, tile_list, pair_mask, tile_count):
    state = pack(positions, velocities, nodal_mass, thickness, pack_index).reshape(-1, 8, 128)
    own = features(connectivity, state)
    ghosts = connectivity.shape[0] // 4
    rim = padded(own[None, None, :, :ghosts], (("wide", 0), ("narrow", 1)))
    around = [rim[i, j] for i in range(3) for j in range(3) if (i, j) != (1, 1)]
    seg_all = jnp.concatenate([own] + around, axis=1)
    force = contact(state, seg_all, tile_list, pair_mask, tile_count, STIFFNESS, DAMPING)
    return scatter(swap(force), pack_index, positions.shape[1])


def solution(mesh):
    return jax.shard_map(
        on_device,
        mesh=mesh,
        in_specs=(
            P(None, AXES),
            P(None, AXES),
            P(AXES),
            P(AXES),
            P(AXES, None),
            P(AXES, None),
            P(None, AXES),
            P(AXES, None),
            P(AXES),
        ),
        out_specs=P(None, AXES),
        check_vma=False,
    )
```

```python
import functools
import jax
import jax.numpy as jnp
from jax import lax
from jax.experimental import pallas as pl
from jax.experimental.pallas import tpu as pltpu
from jax.sharding import PartitionSpec as P

F32 = jnp.float32
BF16 = jnp.bfloat16
I32 = jnp.int32
CHUNK = 512
UNR = 1
GROUP = 4
LOG2E = 1.4426950408889634


def iota(shape, axis):
    return lax.broadcasted_iota(I32, shape, axis)


def split3(x):
    high = x.astype(BF16)
    rest = x - high.astype(F32)
    middle = rest.astype(BF16)
    low = (rest - middle.astype(F32)).astype(BF16)
    return high, middle, low


def expand_rows(tile):
    rows = tile.shape[0]
    high, middle, low = split3(tile)
    parts = [high.astype(F32), middle.astype(F32), low.astype(F32)]
    stacked = jnp.concatenate(parts, axis=0).astype(BF16)
    spread = (iota((3 * rows, 128), 0) % rows == iota((3 * rows, 128), 1) % 8).astype(F32).astype(BF16)
    return lax.dot_general(stacked, spread, (((0,), (0,)), ((), ())), preferred_element_type=F32)


def merge_groups(rows, shape):
    lane = iota(shape, 1)
    bit = 8
    while len(rows) > 1:
        odd = (lane & bit) != 0
        rows = [jnp.where(odd, rows[2 * i + 1], rows[2 * i]) for i in range(len(rows) // 2)]
        bit *= 2
    return rows[0]


def feature_major(rows):
    lane = iota((8, 128), 1)
    pick = (lane // 8) * 8 + iota((8, 128), 0)
    out = None
    for r in range(8):
        moved = jnp.take_along_axis(rows[r], pick, axis=1)
        out = moved if out is None else jnp.where(lane % 8 == r, moved, out)
    return out


def index_chunks(index_ref, body):
    def turn(i, carry):
        body(i, lambda k: index_ref.at[k][i])
        return carry

    lax.fori_loop(0, index_ref.shape[1], turn, 0, unroll=UNR)


def merge_lanes(tiles):
    lane = iota((8, 128), 1)
    bit = 1
    while len(tiles) > 1:
        odd = (lane & bit) != 0
        tiles = [jnp.where(odd, tiles[2 * i + 1], tiles[2 * i]) for i in range(len(tiles) // 2)]
        bit *= 2
    return tiles[0]


def pick_lanes(row_of, lanes, table_ref):
    spread = jnp.broadcast_to(lanes, (8, 128))
    return merge_lanes([jnp.take_along_axis(table_ref[row_of(j)], spread, axis=1) for j in range(128)])


WIDE, NARROW = "wide", "narrow"


def my_place():
    wide, narrow = lax.axis_index(WIDE), lax.axis_index(NARROW)
    return wide // 4, wide % 4, narrow // 2, narrow % 2


def my_number():
    return lax.axis_index(WIDE) * 8 + lax.axis_index(NARROW)


def peer(i):
    z, x, y, core = my_place()
    dz = i % 4
    dx = (i // 4 + i) % 4
    dy = (i // 16 + i // 4 + i) % 4
    dc = (i // 64) % 2
    return ((z + dz) % 4) * 4 + (x + dx) % 4, ((y + dy) % 4) * 2 + (core + dc) % 2


def greet(barrier, peers):
    def one(i, carry):
        pl.semaphore_signal(barrier, inc=1, device_id=peer(i), device_id_type=pl.DeviceIdType.MESH)
        return carry

    lax.fori_loop(1, peers, one, 0)


def block_copy(source_ref, target_ref, send_sem, recv_sem, i):
    wide, narrow = peer(i)
    return pltpu.make_async_remote_copy(
        src_ref=source_ref.at[wide * 8 + narrow],
        dst_ref=target_ref.at[my_number()],
        send_sem=send_sem,
        recv_sem=recv_sem,
        device_id=(wide, narrow),
        device_id_type=pl.DeviceIdType.MESH,
    )


def finish_blocks(source_ref, target_ref, send_sem, recv_sem, peers):
    me = my_number()
    target_ref[me] = source_ref[me]
    rest = pl.ds(0, peers - 1)
    all_of_them = pltpu.make_async_remote_copy(
        src_ref=source_ref.at[rest],
        dst_ref=target_ref.at[rest],
        send_sem=send_sem,
        recv_sem=recv_sem,
        device_id=peer(1),
        device_id_type=pl.DeviceIdType.MESH,
    )
    all_of_them.wait_send()
    all_of_them.wait_recv()


def pack_kernel(
    index_ref, pos_ref, vel_ref, mass_ref, thick_ref, out_ref, rows_ref, stage_ref, send_sem, recv_sem
):
    nodes = pos_ref.shape[1]
    peers = out_ref.shape[0]
    barrier = pltpu.get_barrier_semaphore()
    greet(barrier, peers)

    def fill(b, carry):
        at = pl.ds(pl.multiple_of(b * 128, 128), 128)
        tile = jnp.concatenate([pos_ref[:, at], vel_ref[:, at], mass_ref[:, at], thick_ref[:, at]], axis=0)
        rows_ref[at, :] = expand_rows(tile)
        return carry

    lax.fori_loop(0, nodes // 128, fill, 0, unroll=8)
    rows_ref[nodes : nodes + 8, :] = jnp.zeros((8, 128), F32)
    pl.semaphore_wait(barrier, peers - 1)

    def turn(i, carry):
        wide, narrow = peer((i + 1) % peers)
        number = wide * 8 + narrow
        for part in range(CHUNK // 128):
            lines = []
            for r in range(8):
                got = [rows_ref[pl.ds(index_ref.at[part * 128 + k * 8 + r][number], 1), :] for k in range(16)]
                lines.append(jnp.broadcast_to(merge_groups(got, (1, 128)), (8, 128)))
            stage_ref[number, part] = feature_major(lines)

        @pl.when(i > 0)
        def _():
            block_copy(stage_ref, out_ref, send_sem, recv_sem, i).start()

        return carry

    lax.fori_loop(0, peers, turn, 0)
    finish_blocks(stage_ref, out_ref, send_sem, recv_sem, peers)


VMEM = pl.BlockSpec(memory_space=pltpu.VMEM)
SMEM = pl.BlockSpec(memory_space=pltpu.SMEM)


def columns(pack_index):
    return pack_index.reshape(-1, CHUNK).T


def pack(positions, velocities, nodal_mass, thickness, pack_index):
    nodes = positions.shape[1]
    blocks = (pack_index.shape[1] // CHUNK, CHUNK // 128, 8, 128)
    return pl.pallas_call(
        pack_kernel,
        out_shape=jax.ShapeDtypeStruct(blocks, F32),
        in_specs=[SMEM, VMEM, VMEM, VMEM, VMEM],
        out_specs=VMEM,
        scratch_shapes=[
            pltpu.VMEM((nodes + 8, 128), F32),
            pltpu.VMEM(blocks, F32),
            pltpu.SemaphoreType.DMA,
            pltpu.SemaphoreType.DMA,
        ],
        compiler_params=pltpu.CompilerParams(vmem_limit_bytes=48 << 20, collective_id=0, has_side_effects=True),
        name="pack",
    )(columns(pack_index), positions, velocities, nodal_mass.reshape(1, -1), thickness.reshape(1, -1))


def scatter_kernel(index_ref, force_ref, out_ref, rows_ref, ex_a, ex_b):
    nodes = out_ref.shape[1]
    chunks = index_ref.shape[1]
    tiles = CHUNK // 128

    def spread(c, ex_ref):
        for part in range(tiles):
            ex_ref[part * 128 : part * 128 + 128] = expand_rows(force_ref[c * tiles + part])

    def place(c, ex_ref):
        for j in range(CHUNK):
            rows_ref[pl.ds(index_ref.at[j][c], 1), :] = ex_ref[j : j + 1, :]

    spread(0, ex_a)

    def turn(i, carry):
        spread(2 * i + 1, ex_b)
        place(2 * i, ex_a)
        spread(jnp.minimum(2 * i + 2, chunks - 1), ex_a)
        place(2 * i + 1, ex_b)
        return carry

    lax.fori_loop(0, chunks // 2, turn, 0)

    def collect(b, carry):
        at = pl.multiple_of(b * 128, 128)
        tiles = [rows_ref[pl.ds(at + k * 8, 8), :] for k in range(16)]
        merged = merge_groups(tiles, (8, 128))
        lines = [jnp.broadcast_to(merged[r : r + 1], (8, 128)) for r in range(8)]
        out_ref[:, pl.ds(at, 128)] = feature_major(lines)[0:3]
        return carry

    lax.fori_loop(0, nodes // 128, collect, 0, unroll=8)


def scatter(force, pack_index, nodes):
    return pl.pallas_call(
        scatter_kernel,
        out_shape=jax.ShapeDtypeStruct((3, nodes), F32),
        in_specs=[SMEM, VMEM],
        out_specs=VMEM,
        scratch_shapes=[
            pltpu.VMEM((nodes + 8, 128), F32),
            pltpu.VMEM((CHUNK, 128), F32),
            pltpu.VMEM((CHUNK, 128), F32),
        ],
        compiler_params=pltpu.CompilerParams(vmem_limit_bytes=48 << 20),
        name="scatter",
    )(columns(pack_index), force)


def merge_lanes(tiles):
    lane = iota((8, 128), 1)
    bit = 1
    while len(tiles) > 1:
        odd = (lane & bit) != 0
        tiles = [jnp.where(odd, tiles[2 * i + 1], tiles[2 * i]) for i in range(len(tiles) // 2)]
        bit *= 2
    return tiles[0]


def pick_lanes(row_of, lanes, table_ref):
    spread = jnp.broadcast_to(lanes, (8, 128))
    return merge_lanes([jnp.take_along_axis(table_ref[row_of(j)], spread, axis=1) for j in range(128)])


def features_kernel(row_ref, lane_ref, state_ref, out_ref):
    def chunk(c, carry):
        corner = []
        for i in range(4):
            row_of = lambda q: row_ref.at[i * 128 + q][c]
            corner.append(pick_lanes(row_of, lane_ref[pl.ds(i, 1), pl.ds(pl.multiple_of(c * 128, 128), 128)], state_ref))
        total = (corner[0] + corner[1] + corner[2] + corner[3]) * 0.25
        centre = total[0:3]
        d1 = corner[2] - corner[0]
        d2 = corner[3] - corner[1]
        w0 = d1[1:2] * d2[2:3] - d1[2:3] * d2[1:2]
        w1 = d1[2:3] * d2[0:1] - d1[0:1] * d2[2:3]
        w2 = d1[0:1] * d2[1:2] - d1[1:2] * d2[0:1]
        scale = jnp.maximum(jnp.sqrt(w0 * w0 + w1 * w1 + w2 * w2), 1.0)
        off = [corner[i][0:3] - centre for i in range(4)]
        square = off[0] * off[0] + off[1] * off[1] + off[2] * off[2] + off[3] * off[3]
        spread = (square[0:1] + square[1:2] + square[2:3]) * 0.25
        rows = [centre, w0 / scale, w1 / scale, w2 / scale, total[3:6], spread, jnp.zeros((6, 128), F32)]
        out_ref[:, pl.ds(pl.multiple_of(c * 128, 128), 128)] = jnp.concatenate(rows, axis=0)
        return carry

    lax.fori_loop(0, out_ref.shape[1] // 128, chunk, 0)


def corner_rows(connectivity):
    rows = (connectivity >> 7).T.reshape(4, -1, 128)
    rows = jnp.transpose(rows, (0, 2, 1)).reshape(512, -1)
    return jnp.pad(rows, ((0, 0), (0, 128 - rows.shape[1])))


def features(connectivity, state):
    segs = connectivity.shape[0]
    return pl.pallas_call(
        features_kernel,
        out_shape=jax.ShapeDtypeStruct((16, segs), F32),
        in_specs=[SMEM, VMEM, VMEM],
        out_specs=VMEM,
        compiler_params=pltpu.CompilerParams(vmem_limit_bytes=16 << 20),
        name="features",
    )(corner_rows(connectivity), (connectivity & 127).T, state)


AROUND = [(da, db) for da in (-1, 0, 1) for db in (-1, 0, 1) if (da, db) != (0, 0)]


def ghost_exchange(own_ref, ghost_ref, send_sem, recv_sem):
    wide, narrow = lax.axis_index(WIDE), lax.axis_index(NARROW)
    waits = []
    for k, (da, db) in enumerate(AROUND):
        a, b = wide + da, narrow + db
        inside = (a >= 0) & (a < lax.axis_size(WIDE)) & (b >= 0) & (b < lax.axis_size(NARROW))

        def copy(a=a, b=b, k=k):
            return pltpu.make_async_remote_copy(
                src_ref=own_ref.at[:, pl.ds(0, ghost_ref.shape[2])],
                dst_ref=ghost_ref.at[7 - k],
                send_sem=send_sem.at[k],
                recv_sem=recv_sem.at[7 - k],
                device_id=(a, b),
                device_id_type=pl.DeviceIdType.MESH,
            )

        def arrival(a=a, b=b, k=k):
            return pltpu.make_async_remote_copy(
                src_ref=own_ref.at[:, pl.ds(0, ghost_ref.shape[2])],
                dst_ref=ghost_ref.at[k],
                send_sem=send_sem.at[k],
                recv_sem=recv_sem.at[k],
                device_id=(a, b),
                device_id_type=pl.DeviceIdType.MESH,
            )

        @pl.when(inside)
        def _():
            copy().start()

        @pl.when(jnp.logical_not(inside))
        def _():
            ghost_ref[k] = jnp.zeros(ghost_ref.shape[1:], F32)

        waits.append((inside, arrival))

    def finish():
        for inside, arrival in waits:

            @pl.when(inside)
            def _():
                arrival().wait_send()
                arrival().wait_recv()

    return finish


def contact_kernel(
    tiles_ref,
    entry_ref,
    count_ref,
    state_ref,
    own_ref,
    mask_ref,
    out_ref,
    coef_ref,
    normal_ref,
    keep_a,
    keep_b,
    ghost_ref,
    stage_ref,
    ghost_send,
    ghost_recv,
    send_sem,
    recv_sem,
    *,
    stiffness,
    damping,
):
    blocks = state_ref.shape[0]
    peers = out_ref.shape[0]
    barrier = pltpu.get_barrier_semaphore()
    greet(barrier, peers)

    def prepare(s, f):
        n = f[3:6]
        rate = LOG2E / (f[9:10] + 0.25)
        one = jnp.ones((1, 256), F32)
        zero = jnp.zeros((3, 256), F32)
        dot = lambda a, b: jnp.sum(a * b, axis=0, keepdims=True)
        sides = (
            [-n, dot(f[0:3], n), one],
            [2.0 * rate * f[0:3], -rate * dot(f[0:3], f[0:3]), -rate],
            [-damping * n, damping * dot(f[6:9], n), stiffness * one],
        )
        for i, rows in enumerate(sides):
            high, middle, low = split3(jnp.concatenate(rows + [zero], axis=0))
            coef_ref[s, i] = pack6([high, high, high, middle, middle, low]).T
        high, middle, _ = split3(n)
        gap = zero[0:1]
        normal_ref[s] = jnp.concatenate([high.astype(F32), gap, middle.astype(F32), gap], axis=0)

    own_blocks = own_ref.shape[1] // 256

    def prepare_own(s, carry):
        prepare(s, own_ref[:, pl.ds(pl.multiple_of(s * 256, 256), 256)])
        return carry

    lax.fori_loop(0, own_blocks, prepare_own, 0)
    pl.semaphore_wait(barrier, peers - 1)
    finish_ghosts = ghost_exchange(own_ref, ghost_ref, ghost_send, ghost_recv)
    keep_b[...] = jnp.zeros_like(keep_b)
    finish_ghosts()

    def prepare_ghost(k, carry):
        for half in range(2):
            prepare(own_blocks + 2 * k + half, ghost_ref[k, :, 256 * half : 256 * half + 256])
        return carry

    lax.fori_loop(0, ghost_ref.shape[0], prepare_ghost, 0)
    total = count_ref[0]
    row = iota((8, 128), 0)

    def number(h):
        wide, narrow = peer((h + 1) % peers)
        return wide * 8 + narrow

    def first(block, keep_ref, slot):
        t = entry_ref[block]
        node = state_ref[block]
        sq = jnp.sum(jnp.where(row < 3, node * node, 0.0), axis=0, keepdims=True)
        one = jnp.ones((1, 128), F32)
        zero = jnp.zeros((3, 128), F32)
        sides = (
            [node[0:3], one, node[7:8]],
            [node[0:3], one, sq],
            [node[3:6], one, node[6:7]],
        )
        left = []
        for rows in sides:
            high, middle, low = split3(jnp.concatenate(rows + [zero], axis=0))
            left.append(pack6([high, middle, low, high, middle, high]))
        for half in range(2):
            s = tiles_ref[1, t + half * blocks]
            term = [jnp.dot(coef_ref[s, i], left[i], preferred_element_type=F32) for i in range(3)]
            size = jnp.maximum(term[0], 0.0) * jnp.exp2(term[1]) * term[2]
            top = size.astype(BF16)
            keep_ref[2 * slot + half, 0] = top
            keep_ref[2 * slot + half, 1] = (size - top.astype(F32)).astype(BF16)

    def second(block, keep_ref, slot):
        t = entry_ref[block]
        force = jnp.zeros((8, 128), F32)
        for half in range(2):
            e = t + half * blocks
            live = jnp.where(e < total, 1.0, 0.0)
            mask = mask_ref[pl.ds(e, 1), :].astype(F32) * live
            weights = (normal_ref[tiles_ref[1, e]] * mask).astype(BF16)
            for part in range(2):
                force += jnp.dot(weights, keep_ref[2 * slot + half, part], preferred_element_type=F32)
        return force[0:4] + force[4:8]

    def step(h, before, new_ref, old_ref):
        now, last = number(h), number(before)
        for k in range(GROUP):
            first(now * GROUP + k, new_ref, k)
            stage_ref[last, k] = second(last * GROUP + k, old_ref, k)

    def send(h):
        block_copy(stage_ref, out_ref, send_sem, recv_sem, h + 1).start()

    def turn(i, carry):
        step(2 * i, (2 * i + peers - 1) % peers, keep_a, keep_b)

        @pl.when(i > 0)
        def _():
            send(2 * i - 2)

        step(2 * i + 1, 2 * i, keep_b, keep_a)

        @pl.when(i > 0)
        def _():
            send(2 * i - 1)

        return carry

    lax.fori_loop(0, peers // 2, turn, 0)
    me = my_number()
    for k in range(GROUP):
        stage_ref[me, k] = second(me * GROUP + k, keep_b, k)
    send(peers - 2)
    finish_blocks(stage_ref, out_ref, send_sem, recv_sem, peers)


def pack6(parts):
    return jnp.concatenate([p.astype(F32) for p in parts], axis=0).astype(BF16)


def contact(state, own, tile_list, pair_mask, tile_count, ghosts):
    blocks = state.shape[0]
    seg_blocks = (own.shape[1] + 8 * ghosts) // 256
    back = (blocks // GROUP, GROUP, 4, 128)
    number = jnp.arange(blocks, dtype=I32)
    entry = jnp.sum(jnp.where(tile_list[0:1, :blocks] == number[:, None], number[None], 0), axis=1)
    dma = pltpu.SemaphoreType.DMA
    return pl.pallas_call(
        functools.partial(contact_kernel, stiffness=STIFFNESS, damping=DAMPING),
        out_shape=jax.ShapeDtypeStruct(back, F32),
        in_specs=[SMEM, SMEM, SMEM, VMEM, VMEM, VMEM],
        out_specs=VMEM,
        scratch_shapes=[
            pltpu.VMEM((seg_blocks, 3, 256, 48), BF16),
            pltpu.VMEM((seg_blocks, 8, 256), F32),
            pltpu.VMEM((2 * GROUP, 2, 256, 128), BF16),
            pltpu.VMEM((2 * GROUP, 2, 256, 128), BF16),
            pltpu.VMEM((8, own.shape[0], ghosts), F32),
            pltpu.VMEM(back, F32),
            dma((8,)),
            dma((8,)),
            dma,
            dma,
        ],
        compiler_params=pltpu.CompilerParams(vmem_limit_bytes=32 << 20, collective_id=1, has_side_effects=True),
        name="contact",
    )(tile_list, entry, tile_count, state, own, pair_mask)


STIFFNESS = 1.0
DAMPING = 0.3
AXES = (WIDE, NARROW)


def on_device(positions, velocities, nodal_mass, thickness, pack_index, connectivity, tile_list, pair_mask, tile_count):
    state = pack(positions, velocities, nodal_mass, thickness, pack_index).reshape(-1, 8, 128)
    own = features(connectivity, state)
    force = contact(state, own, tile_list, pair_mask, tile_count, connectivity.shape[0] // 4)
    return scatter(force.reshape(-1, 4, 128), pack_index, positions.shape[1])


def solution(mesh):
    return jax.shard_map(
        on_device,
        mesh=mesh,
        in_specs=(
            P(None, AXES),
            P(None, AXES),
            P(AXES),
            P(AXES),
            P(AXES, None),
            P(AXES, None),
            P(None, AXES),
            P(AXES, None),
            P(AXES),
        ),
        out_specs=P(None, AXES),
        check_vma=False,
    )
```

```python
import functools
import jax
import jax.numpy as jnp
from jax import lax
from jax.experimental import pallas as pl
from jax.experimental.pallas import tpu as pltpu
from jax.sharding import PartitionSpec as P

F32 = jnp.float32
BF16 = jnp.bfloat16
I32 = jnp.int32
CHUNK = 512
UNR = 1
GROUP = 4
LOG2E = 1.4426950408889634


def iota(shape, axis):
    return lax.broadcasted_iota(I32, shape, axis)


def split3(x):
    high = x.astype(BF16)
    rest = x - high.astype(F32)
    middle = rest.astype(BF16)
    low = (rest - middle.astype(F32)).astype(BF16)
    return high, middle, low


def expand_rows(tile):
    rows = tile.shape[0]
    high, middle, low = split3(tile)
    parts = [high.astype(F32), middle.astype(F32), low.astype(F32)]
    stacked = jnp.concatenate(parts, axis=0).astype(BF16)
    spread = (iota((3 * rows, 128), 0) % rows == iota((3 * rows, 128), 1) % 8).astype(F32).astype(BF16)
    return lax.dot_general(stacked, spread, (((0,), (0,)), ((), ())), preferred_element_type=F32)


def merge_groups(rows, shape):
    lane = iota(shape, 1)
    bit = 8
    while len(rows) > 1:
        odd = (lane & bit) != 0
        rows = [jnp.where(odd, rows[2 * i + 1], rows[2 * i]) for i in range(len(rows) // 2)]
        bit *= 2
    return rows[0]


def feature_major(rows):
    lane = iota((8, 128), 1)
    pick = (lane // 8) * 8 + iota((8, 128), 0)
    out = None
    for r in range(8):
        moved = jnp.take_along_axis(rows[r], pick, axis=1)
        out = moved if out is None else jnp.where(lane % 8 == r, moved, out)
    return out


def index_chunks(index_ref, body):
    def turn(i, carry):
        body(i, lambda k: index_ref.at[k][i])
        return carry

    lax.fori_loop(0, index_ref.shape[1], turn, 0, unroll=UNR)


def merge_lanes(tiles):
    lane = iota((8, 128), 1)
    bit = 1
    while len(tiles) > 1:
        odd = (lane & bit) != 0
        tiles = [jnp.where(odd, tiles[2 * i + 1], tiles[2 * i]) for i in range(len(tiles) // 2)]
        bit *= 2
    return tiles[0]


def pick_lanes(row_of, lanes, table_ref):
    spread = jnp.broadcast_to(lanes, (8, 128))
    return merge_lanes([jnp.take_along_axis(table_ref[row_of(j)], spread, axis=1) for j in range(128)])


WIDE, NARROW = "wide", "narrow"


def my_number():
    return lax.axis_index(WIDE) * lax.axis_size(NARROW) + lax.axis_index(NARROW)


def peer(me, i):
    return lax.rem(me + 37 * i, lax.axis_size(WIDE) * lax.axis_size(NARROW))


def place(number):
    return lax.div(number, lax.axis_size(NARROW)), lax.rem(number, lax.axis_size(NARROW))


def greet(barrier, me, peers):
    def one(i, carry):
        pl.semaphore_signal(barrier, inc=1, device_id=place(peer(me, i)), device_id_type=pl.DeviceIdType.MESH)
        return carry

    lax.fori_loop(1, peers, one, 0)


def send_block(source_ref, target_ref, send_sem, recv_sem, me, number):
    pltpu.make_async_remote_copy(
        src_ref=source_ref.at[number],
        dst_ref=target_ref.at[me],
        send_sem=send_sem,
        recv_sem=recv_sem,
        device_id=place(number),
        device_id_type=pl.DeviceIdType.MESH,
    ).start()


def finish_blocks(source_ref, target_ref, send_sem, recv_sem, me, peers):
    target_ref[me] = source_ref[me]
    rest = pl.ds(0, peers - 1)
    all_of_them = pltpu.make_async_remote_copy(
        src_ref=source_ref.at[rest],
        dst_ref=target_ref.at[rest],
        send_sem=send_sem,
        recv_sem=recv_sem,
        device_id=place(peer(me, 1)),
        device_id_type=pl.DeviceIdType.MESH,
    )
    all_of_them.wait_send()
    all_of_them.wait_recv()


def pack_kernel(
    index_ref, pos_ref, vel_ref, mass_ref, thick_ref, out_ref, rows_ref, stage_ref, send_sem, recv_sem
):
    nodes = pos_ref.shape[1]
    peers = out_ref.shape[0]
    me = my_number()
    barrier = pltpu.get_barrier_semaphore()
    greet(barrier, me, peers)

    def fill(b, carry):
        at = pl.ds(pl.multiple_of(b * 128, 128), 128)
        tile = jnp.concatenate([pos_ref[:, at], vel_ref[:, at], mass_ref[:, at], thick_ref[:, at]], axis=0)
        rows_ref[at, :] = expand_rows(tile)
        return carry

    lax.fori_loop(0, nodes // 128, fill, 0, unroll=8)
    rows_ref[nodes : nodes + 8, :] = jnp.zeros((8, 128), F32)
    pl.semaphore_wait(barrier, peers - 1)

    def gather(number, part):
        lines = []
        for r in range(8):
            got = [rows_ref[pl.ds(index_ref.at[part * 128 + k * 8 + r][number], 1), :] for k in range(16)]
            lines.append(jnp.broadcast_to(merge_groups(got, (1, 128)), (8, 128)))
        stage_ref[number, part] = feature_major(lines)

    for part in range(CHUNK // 128):
        gather(peer(me, 1), part)

    def turn(i, carry):
        ready = peer(me, i)
        number = peer(me, i + 1)
        gather(number, 0)
        send_block(stage_ref, out_ref, send_sem, recv_sem, me, ready)
        for part in range(1, CHUNK // 128):
            gather(number, part)
        return carry

    lax.fori_loop(1, peers, turn, 0)
    finish_blocks(stage_ref, out_ref, send_sem, recv_sem, me, peers)


VMEM = pl.BlockSpec(memory_space=pltpu.VMEM)
SMEM = pl.BlockSpec(memory_space=pltpu.SMEM)


def columns(pack_index):
    return pack_index.reshape(-1, CHUNK).T


def pack(positions, velocities, nodal_mass, thickness, pack_index):
    nodes = positions.shape[1]
    blocks = (pack_index.shape[1] // CHUNK, CHUNK // 128, 8, 128)
    return pl.pallas_call(
        pack_kernel,
        out_shape=jax.ShapeDtypeStruct(blocks, F32),
        in_specs=[SMEM, VMEM, VMEM, VMEM, VMEM],
        out_specs=VMEM,
        scratch_shapes=[
            pltpu.VMEM((nodes + 8, 128), F32),
            pltpu.VMEM(blocks, F32),
            pltpu.SemaphoreType.DMA,
            pltpu.SemaphoreType.DMA,
        ],
        compiler_params=pltpu.CompilerParams(vmem_limit_bytes=48 << 20, collective_id=0, has_side_effects=True),
        name="pack",
    )(columns(pack_index), positions, velocities, nodal_mass.reshape(1, -1), thickness.reshape(1, -1))


def scatter_kernel(index_ref, force_ref, out_ref, rows_ref, ex_a, ex_b):
    nodes = out_ref.shape[1]
    chunks = index_ref.shape[1]
    tiles = CHUNK // 128

    def spread(c, ex_ref):
        for part in range(tiles):
            ex_ref[part * 128 : part * 128 + 128] = expand_rows(force_ref[c * tiles + part])

    def place(c, ex_ref):
        for j in range(CHUNK):
            rows_ref[pl.ds(index_ref.at[j][c], 1), :] = ex_ref[j : j + 1, :]

    spread(0, ex_a)

    def turn(i, carry):
        spread(2 * i + 1, ex_b)
        place(2 * i, ex_a)
        spread(jnp.minimum(2 * i + 2, chunks - 1), ex_a)
        place(2 * i + 1, ex_b)
        return carry

    lax.fori_loop(0, chunks // 2, turn, 0)

    def collect(b, carry):
        at = pl.multiple_of(b * 128, 128)
        tiles = [rows_ref[pl.ds(at + k * 8, 8), :] for k in range(16)]
        merged = merge_groups(tiles, (8, 128))
        lines = [jnp.broadcast_to(merged[r : r + 1], (8, 128)) for r in range(8)]
        out_ref[:, pl.ds(at, 128)] = feature_major(lines)[0:3]
        return carry

    lax.fori_loop(0, nodes // 128, collect, 0, unroll=8)


def scatter(force, pack_index, nodes):
    return pl.pallas_call(
        scatter_kernel,
        out_shape=jax.ShapeDtypeStruct((3, nodes), F32),
        in_specs=[SMEM, VMEM],
        out_specs=VMEM,
        scratch_shapes=[
            pltpu.VMEM((nodes + 8, 128), F32),
            pltpu.VMEM((CHUNK, 128), F32),
            pltpu.VMEM((CHUNK, 128), F32),
        ],
        compiler_params=pltpu.CompilerParams(vmem_limit_bytes=48 << 20),
        name="scatter",
    )(columns(pack_index), force)


def merge_lanes(tiles):
    lane = iota((8, 128), 1)
    bit = 1
    while len(tiles) > 1:
        odd = (lane & bit) != 0
        tiles = [jnp.where(odd, tiles[2 * i + 1], tiles[2 * i]) for i in range(len(tiles) // 2)]
        bit *= 2
    return tiles[0]


def pick_lanes(row_of, lanes, table_ref):
    spread = jnp.broadcast_to(lanes, (8, 128))
    return merge_lanes([jnp.take_along_axis(table_ref[row_of(j)], spread, axis=1) for j in range(128)])


def features_kernel(row_ref, lane_ref, state_ref, out_ref):
    def chunk(c, carry):
        corner = []
        for i in range(4):
            row_of = lambda q: row_ref.at[i * 128 + q][c]
            corner.append(pick_lanes(row_of, lane_ref[pl.ds(i, 1), pl.ds(pl.multiple_of(c * 128, 128), 128)], state_ref))
        total = (corner[0] + corner[1] + corner[2] + corner[3]) * 0.25
        centre = total[0:3]
        d1 = corner[2] - corner[0]
        d2 = corner[3] - corner[1]
        w0 = d1[1:2] * d2[2:3] - d1[2:3] * d2[1:2]
        w1 = d1[2:3] * d2[0:1] - d1[0:1] * d2[2:3]
        w2 = d1[0:1] * d2[1:2] - d1[1:2] * d2[0:1]
        scale = jnp.maximum(jnp.sqrt(w0 * w0 + w1 * w1 + w2 * w2), 1.0)
        off = [corner[i][0:3] - centre for i in range(4)]
        square = off[0] * off[0] + off[1] * off[1] + off[2] * off[2] + off[3] * off[3]
        spread = (square[0:1] + square[1:2] + square[2:3]) * 0.25
        rows = [centre, w0 / scale, w1 / scale, w2 / scale, total[3:6], spread, jnp.zeros((6, 128), F32)]
        out_ref[:, pl.ds(pl.multiple_of(c * 128, 128), 128)] = jnp.concatenate(rows, axis=0)
        return carry

    lax.fori_loop(0, out_ref.shape[1] // 128, chunk, 0)


def corner_rows(connectivity):
    rows = (connectivity >> 7).T.reshape(4, -1, 128)
    rows = jnp.transpose(rows, (0, 2, 1)).reshape(512, -1)
    return jnp.pad(rows, ((0, 0), (0, 128 - rows.shape[1])))


def features(connectivity, state):
    segs = connectivity.shape[0]
    return pl.pallas_call(
        features_kernel,
        out_shape=jax.ShapeDtypeStruct((16, segs), F32),
        in_specs=[SMEM, VMEM, VMEM],
        out_specs=VMEM,
        compiler_params=pltpu.CompilerParams(vmem_limit_bytes=16 << 20),
        name="features",
    )(corner_rows(connectivity), (connectivity & 127).T, state)


AROUND = [(da, db) for da in (-1, 0, 1) for db in (-1, 0, 1) if (da, db) != (0, 0)]


def ghost_exchange(own_ref, ghost_ref, send_sem, recv_sem):
    wide, narrow = lax.axis_index(WIDE), lax.axis_index(NARROW)
    waits = []
    for k, (da, db) in enumerate(AROUND):
        a, b = wide + da, narrow + db
        inside = (a >= 0) & (a < lax.axis_size(WIDE)) & (b >= 0) & (b < lax.axis_size(NARROW))

        def copy(a=a, b=b, k=k):
            return pltpu.make_async_remote_copy(
                src_ref=own_ref.at[:, pl.ds(0, ghost_ref.shape[2])],
                dst_ref=ghost_ref.at[7 - k],
                send_sem=send_sem.at[k],
                recv_sem=recv_sem.at[7 - k],
                device_id=(a, b),
                device_id_type=pl.DeviceIdType.MESH,
            )

        def arrival(a=a, b=b, k=k):
            return pltpu.make_async_remote_copy(
                src_ref=own_ref.at[:, pl.ds(0, ghost_ref.shape[2])],
                dst_ref=ghost_ref.at[k],
                send_sem=send_sem.at[k],
                recv_sem=recv_sem.at[k],
                device_id=(a, b),
                device_id_type=pl.DeviceIdType.MESH,
            )

        @pl.when(inside)
        def _():
            copy().start()

        @pl.when(jnp.logical_not(inside))
        def _():
            ghost_ref[k] = jnp.zeros(ghost_ref.shape[1:], F32)

        waits.append((inside, arrival))

    def finish():
        for inside, arrival in waits:

            @pl.when(inside)
            def _():
                arrival().wait_send()
                arrival().wait_recv()

    return finish


def contact_kernel(
    tiles_ref,
    entry_ref,
    count_ref,
    state_ref,
    own_ref,
    mask_ref,
    out_ref,
    coef_ref,
    normal_ref,
    keep_a,
    keep_b,
    ghost_ref,
    stage_ref,
    ghost_send,
    ghost_recv,
    send_sem,
    recv_sem,
    *,
    stiffness,
    damping,
):
    blocks = state_ref.shape[0]
    peers = out_ref.shape[0]
    me = my_number()
    barrier = pltpu.get_barrier_semaphore()
    greet(barrier, me, peers)

    def prepare(s, f):
        n = f[3:6]
        rate = LOG2E / (f[9:10] + 0.25)
        one = jnp.ones((1, 256), F32)
        zero = jnp.zeros((3, 256), F32)
        dot = lambda a, b: jnp.sum(a * b, axis=0, keepdims=True)
        sides = (
            [-n, dot(f[0:3], n), one],
            [2.0 * rate * f[0:3], -rate * dot(f[0:3], f[0:3]), -rate],
            [-damping * n, damping * dot(f[6:9], n), stiffness * one],
        )
        for i, rows in enumerate(sides):
            high, middle, low = split3(jnp.concatenate(rows + [zero], axis=0))
            coef_ref[s, i] = pack6([high, high, high, middle, middle, low]).T
        high, middle, _ = split3(n)
        gap = zero[0:1]
        normal_ref[s] = jnp.concatenate([high.astype(F32), gap, middle.astype(F32), gap], axis=0)

    own_blocks = own_ref.shape[1] // 256

    def prepare_own(s, carry):
        prepare(s, own_ref[:, pl.ds(pl.multiple_of(s * 256, 256), 256)])
        return carry

    lax.fori_loop(0, own_blocks, prepare_own, 0)
    pl.semaphore_wait(barrier, peers - 1)
    finish_ghosts = ghost_exchange(own_ref, ghost_ref, ghost_send, ghost_recv)
    finish_ghosts()

    def prepare_ghost(k, carry):
        for half in range(2):
            prepare(own_blocks + 2 * k + half, ghost_ref[k, :, 256 * half : 256 * half + 256])
        return carry

    lax.fori_loop(0, ghost_ref.shape[0], prepare_ghost, 0)
    total = count_ref[0]
    row = iota((8, 128), 0)

    def first(block, keep_ref, slot):
        t = entry_ref[block]
        node = state_ref[block]
        sq = jnp.sum(jnp.where(row < 3, node * node, 0.0), axis=0, keepdims=True)
        one = jnp.ones((1, 128), F32)
        zero = jnp.zeros((3, 128), F32)
        sides = (
            [node[0:3], one, node[7:8]],
            [node[0:3], one, sq],
            [node[3:6], one, node[6:7]],
        )
        left = []
        for rows in sides:
            high, middle, low = split3(jnp.concatenate(rows + [zero], axis=0))
            left.append(pack6([high, middle, low, high, middle, high]))
        for half in range(2):
            s = tiles_ref[1, t + half * blocks]
            term = [jnp.dot(coef_ref[s, i], left[i], preferred_element_type=F32) for i in range(3)]
            size = jnp.maximum(term[0], 0.0) * jnp.exp2(term[1]) * term[2]
            top = size.astype(BF16)
            keep_ref[2 * slot + half, 0] = top
            keep_ref[2 * slot + half, 1] = (size - top.astype(F32)).astype(BF16)

    def second(block, keep_ref, slot):
        t = entry_ref[block]
        force = jnp.zeros((8, 128), F32)
        for half in range(2):
            e = t + half * blocks
            live = jnp.where(e < total, 1.0, 0.0)
            mask = mask_ref[pl.ds(e, 1), :].astype(F32) * live
            weights = (normal_ref[tiles_ref[1, e]] * mask).astype(BF16)
            for part in range(2):
                force += jnp.dot(weights, keep_ref[2 * slot + half, part], preferred_element_type=F32)
        return force[0:4] + force[4:8]

    def step(now, last, new_ref, old_ref, send=None):
        for k in range(GROUP):
            first(now * GROUP + k, new_ref, k)
            if last is not None:
                stage_ref[last, k] = second(last * GROUP + k, old_ref, k)
            if k == 0 and send is not None:
                send_block(stage_ref, out_ref, send_sem, recv_sem, me, send)

    step(peer(me, 1), None, keep_a, keep_b)
    step(peer(me, 2), peer(me, 1), keep_b, keep_a)

    def turn(i, carry):
        a, b, c, d = (peer(me, 2 * i + j) for j in (-1, 0, 1, 2))
        step(c, b, keep_a, keep_b, a)
        step(d, c, keep_b, keep_a, b)
        return carry

    lax.fori_loop(1, peers // 2, turn, 0)
    last = peer(me, peers - 1)
    for k in range(GROUP):
        stage_ref[me, k] = second(me * GROUP + k, keep_b, k)
    send_block(stage_ref, out_ref, send_sem, recv_sem, me, last)
    finish_blocks(stage_ref, out_ref, send_sem, recv_sem, me, peers)


def pack6(parts):
    return jnp.concatenate([p.astype(F32) for p in parts], axis=0).astype(BF16)


def contact(state, own, tile_list, pair_mask, tile_count, ghosts):
    blocks = state.shape[0]
    seg_blocks = (own.shape[1] + 8 * ghosts) // 256
    back = (blocks // GROUP, GROUP, 4, 128)
    number = jnp.arange(blocks, dtype=I32)
    entry = jnp.sum(jnp.where(tile_list[0:1, :blocks] == number[:, None], number[None], 0), axis=1)
    dma = pltpu.SemaphoreType.DMA
    return pl.pallas_call(
        functools.partial(contact_kernel, stiffness=STIFFNESS, damping=DAMPING),
        out_shape=jax.ShapeDtypeStruct(back, F32),
        in_specs=[SMEM, SMEM, SMEM, VMEM, VMEM, VMEM],
        out_specs=VMEM,
        scratch_shapes=[
            pltpu.VMEM((seg_blocks, 3, 256, 48), BF16),
            pltpu.VMEM((seg_blocks, 8, 256), F32),
            pltpu.VMEM((2 * GROUP, 2, 256, 128), BF16),
            pltpu.VMEM((2 * GROUP, 2, 256, 128), BF16),
            pltpu.VMEM((8, own.shape[0], ghosts), F32),
            pltpu.VMEM(back, F32),
            dma((8,)),
            dma((8,)),
            dma,
            dma,
        ],
        compiler_params=pltpu.CompilerParams(vmem_limit_bytes=32 << 20, collective_id=1, has_side_effects=True),
        name="contact",
    )(tile_list, entry, tile_count, state, own, pair_mask)


STIFFNESS = 1.0
DAMPING = 0.3
AXES = (WIDE, NARROW)


def on_device(positions, velocities, nodal_mass, thickness, pack_index, connectivity, tile_list, pair_mask, tile_count):
    state = pack(positions, velocities, nodal_mass, thickness, pack_index).reshape(-1, 8, 128)
    own = features(connectivity, state)
    force = contact(state, own, tile_list, pair_mask, tile_count, connectivity.shape[0] // 4)
    return scatter(force.reshape(-1, 4, 128), pack_index, positions.shape[1])


def solution(mesh):
    return jax.shard_map(
        on_device,
        mesh=mesh,
        in_specs=(
            P(None, AXES),
            P(None, AXES),
            P(AXES),
            P(AXES),
            P(AXES, None),
            P(AXES, None),
            P(None, AXES),
            P(AXES, None),
            P(AXES),
        ),
        out_specs=P(None, AXES),
        check_vma=False,
    )
```

```python
import functools
import jax
import jax.numpy as jnp
from jax import lax
from jax.experimental import pallas as pl
from jax.experimental.pallas import tpu as pltpu
from jax.sharding import PartitionSpec as P

F32 = jnp.float32
BF16 = jnp.bfloat16
I32 = jnp.int32
CHUNK = 512
UNR = 1
GROUP = 4
LOG2E = 1.4426950408889634


def iota(shape, axis):
    return lax.broadcasted_iota(I32, shape, axis)


def split3(x):
    high = x.astype(BF16)
    rest = x - high.astype(F32)
    middle = rest.astype(BF16)
    low = (rest - middle.astype(F32)).astype(BF16)
    return high, middle, low


def expand_rows(tile):
    rows = tile.shape[0]
    high, middle, low = split3(tile)
    parts = [high.astype(F32), middle.astype(F32), low.astype(F32)]
    stacked = jnp.concatenate(parts, axis=0).astype(BF16)
    spread = (iota((3 * rows, 128), 0) % rows == iota((3 * rows, 128), 1) % 8).astype(F32).astype(BF16)
    return lax.dot_general(stacked, spread, (((0,), (0,)), ((), ())), preferred_element_type=F32)


def merge_groups(rows, shape):
    lane = iota(shape, 1)
    bit = 8
    while len(rows) > 1:
        odd = (lane & bit) != 0
        rows = [jnp.where(odd, rows[2 * i + 1], rows[2 * i]) for i in range(len(rows) // 2)]
        bit *= 2
    return rows[0]


def feature_major(rows):
    lane = iota((8, 128), 1)
    pick = (lane // 8) * 8 + iota((8, 128), 0)
    out = None
    for r in range(8):
        moved = jnp.take_along_axis(rows[r], pick, axis=1)
        out = moved if out is None else jnp.where(lane % 8 == r, moved, out)
    return out


def index_chunks(index_ref, body):
    def turn(i, carry):
        body(i, lambda k: index_ref.at[k][i])
        return carry

    lax.fori_loop(0, index_ref.shape[1], turn, 0, unroll=UNR)


def merge_lanes(tiles):
    lane = iota((8, 128), 1)
    bit = 1
    while len(tiles) > 1:
        odd = (lane & bit) != 0
        tiles = [jnp.where(odd, tiles[2 * i + 1], tiles[2 * i]) for i in range(len(tiles) // 2)]
        bit *= 2
    return tiles[0]


def pick_lanes(row_of, lanes, table_ref):
    spread = jnp.broadcast_to(lanes, (8, 128))
    return merge_lanes([jnp.take_along_axis(table_ref[row_of(j)], spread, axis=1) for j in range(128)])


WIDE, NARROW = "wide", "narrow"


def my_number():
    return lax.axis_index(WIDE) * lax.axis_size(NARROW) + lax.axis_index(NARROW)


def peer(me, i):
    return lax.rem(me + 37 * i, lax.axis_size(WIDE) * lax.axis_size(NARROW))


def place(number):
    return lax.div(number, lax.axis_size(NARROW)), lax.rem(number, lax.axis_size(NARROW))


def greet(barrier, me, i):
    pl.semaphore_signal(barrier, inc=1, device_id=place(peer(me, i)), device_id_type=pl.DeviceIdType.MESH)


def send_block(source_ref, target_ref, send_sem, recv_sem, me, number):
    pltpu.make_async_remote_copy(
        src_ref=source_ref.at[number],
        dst_ref=target_ref.at[me],
        send_sem=send_sem,
        recv_sem=recv_sem,
        device_id=place(number),
        device_id_type=pl.DeviceIdType.MESH,
    ).start()


def finish_blocks(source_ref, target_ref, send_sem, recv_sem, me, peers):
    target_ref[me] = source_ref[me]
    rest = pl.ds(0, peers - 1)
    all_of_them = pltpu.make_async_remote_copy(
        src_ref=source_ref.at[rest],
        dst_ref=target_ref.at[rest],
        send_sem=send_sem,
        recv_sem=recv_sem,
        device_id=place(peer(me, 1)),
        device_id_type=pl.DeviceIdType.MESH,
    )
    all_of_them.wait_send()
    all_of_them.wait_recv()


def pack_kernel(
    index_ref, pos_ref, vel_ref, mass_ref, thick_ref, out_ref, rows_ref, stage_ref, send_sem, recv_sem
):
    nodes = pos_ref.shape[1]
    peers = out_ref.shape[0]
    me = my_number()
    barrier = pltpu.get_barrier_semaphore()

    def fill(b):
        at = pl.ds(pl.multiple_of(b * 128, 128), 128)
        tile = jnp.concatenate([pos_ref[:, at], vel_ref[:, at], mass_ref[:, at], thick_ref[:, at]], axis=0)
        rows_ref[at, :] = expand_rows(tile)

    share = 2 * (nodes // 128) // peers

    def fill_and_greet(i, carry):
        for k in range(share):
            fill(i * share + k)
        greet(barrier, me, 2 * i + 1)
        greet(barrier, me, 2 * i + 2)
        return carry

    lax.fori_loop(0, peers // 2 - 1, fill_and_greet, 0)
    greet(barrier, me, peers - 1)
    for k in range(share):
        fill((peers // 2 - 1) * share + k)
    rows_ref[nodes : nodes + 8, :] = jnp.zeros((8, 128), F32)
    pl.semaphore_wait(barrier, peers - 1)

    def gather(number, part):
        lines = []
        for r in range(8):
            got = [rows_ref[pl.ds(index_ref.at[part * 128 + k * 8 + r][number], 1), :] for k in range(16)]
            lines.append(jnp.broadcast_to(merge_groups(got, (1, 128)), (8, 128)))
        stage_ref[number, part] = feature_major(lines)

    for part in range(CHUNK // 128):
        gather(peer(me, 1), part)

    def turn(i, carry):
        ready = peer(me, i)
        number = peer(me, i + 1)
        gather(number, 0)
        send_block(stage_ref, out_ref, send_sem, recv_sem, me, ready)
        for part in range(1, CHUNK // 128):
            gather(number, part)
        return carry

    lax.fori_loop(1, peers, turn, 0)
    finish_blocks(stage_ref, out_ref, send_sem, recv_sem, me, peers)


VMEM = pl.BlockSpec(memory_space=pltpu.VMEM)
SMEM = pl.BlockSpec(memory_space=pltpu.SMEM)


def columns(pack_index):
    return pack_index.reshape(-1, CHUNK).T


def pack(positions, velocities, nodal_mass, thickness, pack_index):
    nodes = positions.shape[1]
    blocks = (pack_index.shape[1] // CHUNK, CHUNK // 128, 8, 128)
    return pl.pallas_call(
        pack_kernel,
        out_shape=jax.ShapeDtypeStruct(blocks, F32),
        in_specs=[SMEM, VMEM, VMEM, VMEM, VMEM],
        out_specs=VMEM,
        scratch_shapes=[
            pltpu.VMEM((nodes + 8, 128), F32),
            pltpu.VMEM(blocks, F32),
            pltpu.SemaphoreType.DMA,
            pltpu.SemaphoreType.DMA,
        ],
        compiler_params=pltpu.CompilerParams(vmem_limit_bytes=48 << 20, collective_id=0, has_side_effects=True),
        name="pack",
    )(columns(pack_index), positions, velocities, nodal_mass.reshape(1, -1), thickness.reshape(1, -1))


def scatter_kernel(index_ref, force_ref, out_ref, rows_ref, ex_a, ex_b):
    nodes = out_ref.shape[1]
    chunks = index_ref.shape[1]
    tiles = CHUNK // 128

    def spread(c, ex_ref):
        for part in range(tiles):
            ex_ref[part * 128 : part * 128 + 128] = expand_rows(force_ref[c * tiles + part])

    def place(c, ex_ref):
        for j in range(CHUNK):
            rows_ref[pl.ds(index_ref.at[j][c], 1), :] = ex_ref[j : j + 1, :]

    spread(0, ex_a)

    def turn(i, carry):
        spread(2 * i + 1, ex_b)
        place(2 * i, ex_a)
        spread(jnp.minimum(2 * i + 2, chunks - 1), ex_a)
        place(2 * i + 1, ex_b)
        return carry

    lax.fori_loop(0, chunks // 2, turn, 0)

    def collect(b, carry):
        at = pl.multiple_of(b * 128, 128)
        tiles = [rows_ref[pl.ds(at + k * 8, 8), :] for k in range(16)]
        merged = merge_groups(tiles, (8, 128))
        lines = [jnp.broadcast_to(merged[r : r + 1], (8, 128)) for r in range(8)]
        out_ref[:, pl.ds(at, 128)] = feature_major(lines)[0:3]
        return carry

    lax.fori_loop(0, nodes // 128, collect, 0, unroll=8)


def scatter(force, pack_index, nodes):
    return pl.pallas_call(
        scatter_kernel,
        out_shape=jax.ShapeDtypeStruct((3, nodes), F32),
        in_specs=[SMEM, VMEM],
        out_specs=VMEM,
        scratch_shapes=[
            pltpu.VMEM((nodes + 8, 128), F32),
            pltpu.VMEM((CHUNK, 128), F32),
            pltpu.VMEM((CHUNK, 128), F32),
        ],
        compiler_params=pltpu.CompilerParams(vmem_limit_bytes=48 << 20),
        name="scatter",
    )(columns(pack_index), force)


def merge_lanes(tiles):
    lane = iota((8, 128), 1)
    bit = 1
    while len(tiles) > 1:
        odd = (lane & bit) != 0
        tiles = [jnp.where(odd, tiles[2 * i + 1], tiles[2 * i]) for i in range(len(tiles) // 2)]
        bit *= 2
    return tiles[0]


def pick_lanes(row_of, lanes, table_ref):
    spread = jnp.broadcast_to(lanes, (8, 128))
    return merge_lanes([jnp.take_along_axis(table_ref[row_of(j)], spread, axis=1) for j in range(128)])


def segment_features(c, row_ref, lane_ref, state_ref, out_ref):
    corner = []
    for i in range(4):
        row_of = lambda q: row_ref.at[i * 128 + q][c]
        corner.append(pick_lanes(row_of, lane_ref[pl.ds(i, 1), pl.ds(pl.multiple_of(c * 128, 128), 128)], state_ref))
    total = (corner[0] + corner[1] + corner[2] + corner[3]) * 0.25
    centre = total[0:3]
    d1 = corner[2] - corner[0]
    d2 = corner[3] - corner[1]
    w0 = d1[1:2] * d2[2:3] - d1[2:3] * d2[1:2]
    w1 = d1[2:3] * d2[0:1] - d1[0:1] * d2[2:3]
    w2 = d1[0:1] * d2[1:2] - d1[1:2] * d2[0:1]
    scale = jnp.maximum(jnp.sqrt(w0 * w0 + w1 * w1 + w2 * w2), 1.0)
    off = [corner[i][0:3] - centre for i in range(4)]
    square = off[0] * off[0] + off[1] * off[1] + off[2] * off[2] + off[3] * off[3]
    spread = (square[0:1] + square[1:2] + square[2:3]) * 0.25
    rows = [centre, w0 / scale, w1 / scale, w2 / scale, total[3:6], spread, jnp.zeros((6, 128), F32)]
    out_ref[:, pl.ds(pl.multiple_of(c * 128, 128), 128)] = jnp.concatenate(rows, axis=0)


def corner_rows(connectivity):
    rows = (connectivity >> 7).T.reshape(4, -1, 128)
    rows = jnp.transpose(rows, (0, 2, 1)).reshape(512, -1)
    return jnp.pad(rows, ((0, 0), (0, 128 - rows.shape[1])))


AROUND = [(da, db) for da in (-1, 0, 1) for db in (-1, 0, 1) if (da, db) != (0, 0)]


def ghost_exchange(own_ref, ghost_ref, send_sem, recv_sem):
    wide, narrow = lax.axis_index(WIDE), lax.axis_index(NARROW)
    waits = []
    for k, (da, db) in enumerate(AROUND):
        a, b = wide + da, narrow + db
        inside = (a >= 0) & (a < lax.axis_size(WIDE)) & (b >= 0) & (b < lax.axis_size(NARROW))

        def copy(a=a, b=b, k=k):
            return pltpu.make_async_remote_copy(
                src_ref=own_ref.at[:, pl.ds(0, ghost_ref.shape[2])],
                dst_ref=ghost_ref.at[7 - k],
                send_sem=send_sem.at[k],
                recv_sem=recv_sem.at[7 - k],
                device_id=(a, b),
                device_id_type=pl.DeviceIdType.MESH,
            )

        def arrival(a=a, b=b, k=k):
            return pltpu.make_async_remote_copy(
                src_ref=own_ref.at[:, pl.ds(0, ghost_ref.shape[2])],
                dst_ref=ghost_ref.at[k],
                send_sem=send_sem.at[k],
                recv_sem=recv_sem.at[k],
                device_id=(a, b),
                device_id_type=pl.DeviceIdType.MESH,
            )

        @pl.when(inside)
        def _():
            copy().start()

        @pl.when(jnp.logical_not(inside))
        def _():
            ghost_ref[k] = jnp.zeros(ghost_ref.shape[1:], F32)

        waits.append((inside, arrival))

    def finish():
        for inside, arrival in waits:

            @pl.when(inside)
            def _():
                arrival().wait_send()
                arrival().wait_recv()

    return finish


def contact_kernel(
    tiles_ref,
    entry_ref,
    count_ref,
    row_ref,
    lane_ref,
    state_ref,
    mask_ref,
    out_ref,
    own_ref,
    coef_ref,
    normal_ref,
    keep_a,
    keep_b,
    ghost_ref,
    stage_ref,
    ghost_send,
    ghost_recv,
    send_sem,
    recv_sem,
    *,
    stiffness,
    damping,
):
    blocks = state_ref.shape[0]
    peers = out_ref.shape[0]
    me = my_number()
    barrier = pltpu.get_barrier_semaphore()

    def corners(c, carry):
        segment_features(c, row_ref, lane_ref, state_ref, own_ref)
        return carry

    ghost_chunks = ghost_ref.shape[2] // 128
    first_ones = 1 + (peers - 1) % ghost_chunks
    for i in range(1, first_ones):
        greet(barrier, me, i)
    share = (peers - first_ones) // ghost_chunks

    def corners_and_greet(c, carry):
        for j in range(share):
            greet(barrier, me, first_ones + c * share + j)
        return corners(c, carry)

    lax.fori_loop(0, ghost_chunks, corners_and_greet, 0)
    lax.fori_loop(ghost_chunks, ghost_chunks + 2, corners, 0)
    pl.semaphore_wait(barrier, peers - 1)
    finish_ghosts = ghost_exchange(own_ref, ghost_ref, ghost_send, ghost_recv)
    lax.fori_loop(ghost_chunks + 2, own_ref.shape[1] // 128, corners, 0)

    def prepare(s, f):
        n = f[3:6]
        rate = LOG2E / (f[9:10] + 0.25)
        one = jnp.ones((1, 256), F32)
        zero = jnp.zeros((3, 256), F32)
        dot = lambda a, b: jnp.sum(a * b, axis=0, keepdims=True)
        sides = (
            [-n, dot(f[0:3], n), one],
            [2.0 * rate * f[0:3], -rate * dot(f[0:3], f[0:3]), -rate],
            [-damping * n, damping * dot(f[6:9], n), stiffness * one],
        )
        for i, rows in enumerate(sides):
            high, middle, low = split3(jnp.concatenate(rows + [zero], axis=0))
            coef_ref[s, i] = pack6([high, high, high, middle, middle, low]).T
        high, middle, _ = split3(n)
        gap = zero[0:1]
        normal_ref[s] = jnp.concatenate([high.astype(F32), gap, middle.astype(F32), gap], axis=0)

    own_blocks = own_ref.shape[1] // 256

    def prepare_own(s, carry):
        prepare(s, own_ref[:, pl.ds(pl.multiple_of(s * 256, 256), 256)])
        return carry

    lax.fori_loop(0, own_blocks, prepare_own, 0)
    finish_ghosts()

    def prepare_ghost(k, carry):
        for half in range(2):
            prepare(own_blocks + 2 * k + half, ghost_ref[k, :, 256 * half : 256 * half + 256])
        return carry

    lax.fori_loop(0, ghost_ref.shape[0], prepare_ghost, 0)
    total = count_ref[0]
    row = iota((8, 128), 0)

    def first(block, keep_ref, slot):
        t = entry_ref[block]
        node = state_ref[block]
        sq = jnp.sum(jnp.where(row < 3, node * node, 0.0), axis=0, keepdims=True)
        one = jnp.ones((1, 128), F32)
        zero = jnp.zeros((3, 128), F32)
        sides = (
            [node[0:3], one, node[7:8]],
            [node[0:3], one, sq],
            [node[3:6], one, node[6:7]],
        )
        left = []
        for rows in sides:
            high, middle, low = split3(jnp.concatenate(rows + [zero], axis=0))
            left.append(pack6([high, middle, low, high, middle, high]))
        for half in range(2):
            s = tiles_ref[1, t + half * blocks]
            term = [jnp.dot(coef_ref[s, i], left[i], preferred_element_type=F32) for i in range(3)]
            size = jnp.maximum(term[0], 0.0) * jnp.exp2(term[1]) * term[2]
            top = size.astype(BF16)
            keep_ref[2 * slot + half, 0] = top
            keep_ref[2 * slot + half, 1] = (size - top.astype(F32)).astype(BF16)

    def second(block, keep_ref, slot):
        t = entry_ref[block]
        force = jnp.zeros((8, 128), F32)
        for half in range(2):
            e = t + half * blocks
            live = jnp.where(e < total, 1.0, 0.0)
            mask = mask_ref[pl.ds(e, 1), :].astype(F32) * live
            weights = (normal_ref[tiles_ref[1, e]] * mask).astype(BF16)
            for part in range(2):
                force += jnp.dot(weights, keep_ref[2 * slot + half, part], preferred_element_type=F32)
        return force[0:4] + force[4:8]

    def step(now, last, new_ref, old_ref, send=None):
        for k in range(GROUP):
            first(now * GROUP + k, new_ref, k)
            if last is not None:
                stage_ref[last, k] = second(last * GROUP + k, old_ref, k)
            if k == 0 and send is not None:
                send_block(stage_ref, out_ref, send_sem, recv_sem, me, send)

    step(peer(me, 1), None, keep_a, keep_b)
    step(peer(me, 2), peer(me, 1), keep_b, keep_a)

    def turn(i, carry):
        a, b, c, d = (peer(me, 2 * i + j) for j in (-1, 0, 1, 2))
        step(c, b, keep_a, keep_b, a)
        step(d, c, keep_b, keep_a, b)
        return carry

    lax.fori_loop(1, peers // 2, turn, 0)
    last = peer(me, peers - 1)
    for k in range(GROUP):
        stage_ref[me, k] = second(me * GROUP + k, keep_b, k)
    send_block(stage_ref, out_ref, send_sem, recv_sem, me, last)
    finish_blocks(stage_ref, out_ref, send_sem, recv_sem, me, peers)


def pack6(parts):
    return jnp.concatenate([p.astype(F32) for p in parts], axis=0).astype(BF16)


def contact(state, connectivity, tile_list, pair_mask, tile_count):
    blocks = state.shape[0]
    segs = connectivity.shape[0]
    ghosts = segs // 4
    seg_blocks = (segs + 8 * ghosts) // 256
    back = (blocks // GROUP, GROUP, 4, 128)
    number = jnp.arange(blocks, dtype=I32)
    entry = jnp.sum(jnp.where(tile_list[0:1, :blocks] == number[:, None], number[None], 0), axis=1)
    dma = pltpu.SemaphoreType.DMA
    return pl.pallas_call(
        functools.partial(contact_kernel, stiffness=STIFFNESS, damping=DAMPING),
        out_shape=jax.ShapeDtypeStruct(back, F32),
        in_specs=[SMEM, SMEM, SMEM, SMEM, VMEM, VMEM, VMEM],
        out_specs=VMEM,
        scratch_shapes=[
            pltpu.VMEM((16, segs), F32),
            pltpu.VMEM((seg_blocks, 3, 256, 48), BF16),
            pltpu.VMEM((seg_blocks, 8, 256), F32),
            pltpu.VMEM((2 * GROUP, 2, 256, 128), BF16),
            pltpu.VMEM((2 * GROUP, 2, 256, 128), BF16),
            pltpu.VMEM((8, 16, ghosts), F32),
            pltpu.VMEM(back, F32),
            dma((8,)),
            dma((8,)),
            dma,
            dma,
        ],
        compiler_params=pltpu.CompilerParams(vmem_limit_bytes=32 << 20, collective_id=1, has_side_effects=True),
        name="contact",
    )(tile_list, entry, tile_count, corner_rows(connectivity), (connectivity & 127).T, state, pair_mask)


STIFFNESS = 1.0
DAMPING = 0.3
AXES = (WIDE, NARROW)


def on_device(positions, velocities, nodal_mass, thickness, pack_index, connectivity, tile_list, pair_mask, tile_count):
    state = pack(positions, velocities, nodal_mass, thickness, pack_index).reshape(-1, 8, 128)
    force = contact(state, connectivity, tile_list, pair_mask, tile_count)
    return scatter(force.reshape(-1, 4, 128), pack_index, positions.shape[1])


def solution(mesh):
    return jax.shard_map(
        on_device,
        mesh=mesh,
        in_specs=(
            P(None, AXES),
            P(None, AXES),
            P(AXES),
            P(AXES),
            P(AXES, None),
            P(AXES, None),
            P(None, AXES),
            P(AXES, None),
            P(AXES),
        ),
        out_specs=P(None, AXES),
        check_vma=False,
    )
```

```python
import functools
import jax
import jax.numpy as jnp
from jax import lax
from jax.experimental import pallas as pl
from jax.experimental.pallas import tpu as pltpu
from jax.sharding import PartitionSpec as P

F32 = jnp.float32
BF16 = jnp.bfloat16
I32 = jnp.int32
CHUNK = 512
UNR = 1
GROUP = 4
LOG2E = 1.4426950408889634


def iota(shape, axis):
    return lax.broadcasted_iota(I32, shape, axis)


def split3(x):
    high = x.astype(BF16)
    rest = x - high.astype(F32)
    middle = rest.astype(BF16)
    low = (rest - middle.astype(F32)).astype(BF16)
    return high, middle, low


def expand_rows(tile):
    rows = tile.shape[0]
    high, middle, low = split3(tile)
    parts = [high.astype(F32), middle.astype(F32), low.astype(F32)]
    stacked = jnp.concatenate(parts, axis=0).astype(BF16)
    spread = (iota((3 * rows, 128), 0) % rows == iota((3 * rows, 128), 1) % 8).astype(F32).astype(BF16)
    return lax.dot_general(stacked, spread, (((0,), (0,)), ((), ())), preferred_element_type=F32)


def merge_groups(rows, shape):
    lane = iota(shape, 1)
    bit = 8
    while len(rows) > 1:
        odd = (lane & bit) != 0
        rows = [jnp.where(odd, rows[2 * i + 1], rows[2 * i]) for i in range(len(rows) // 2)]
        bit *= 2
    return rows[0]


def feature_major(rows):
    lane = iota((8, 128), 1)
    pick = (lane // 8) * 8 + iota((8, 128), 0)
    out = None
    for r in range(8):
        moved = jnp.take_along_axis(rows[r], pick, axis=1)
        out = moved if out is None else jnp.where(lane % 8 == r, moved, out)
    return out


def index_chunks(index_ref, body):
    def turn(i, carry):
        body(i, lambda k: index_ref.at[k][i])
        return carry

    lax.fori_loop(0, index_ref.shape[1], turn, 0, unroll=UNR)


def merge_lanes(tiles):
    lane = iota((8, 128), 1)
    bit = 1
    while len(tiles) > 1:
        odd = (lane & bit) != 0
        tiles = [jnp.where(odd, tiles[2 * i + 1], tiles[2 * i]) for i in range(len(tiles) // 2)]
        bit *= 2
    return tiles[0]


def pick_lanes(row_of, lanes, table_ref):
    spread = jnp.broadcast_to(lanes, (8, 128))
    return merge_lanes([jnp.take_along_axis(table_ref[row_of(j)], spread, axis=1) for j in range(128)])


WIDE, NARROW = "wide", "narrow"


def my_number():
    return lax.axis_index(WIDE) * lax.axis_size(NARROW) + lax.axis_index(NARROW)


def peer(me, i):
    return lax.rem(me + 37 * i, lax.axis_size(WIDE) * lax.axis_size(NARROW))


def place(number):
    return lax.div(number, lax.axis_size(NARROW)), lax.rem(number, lax.axis_size(NARROW))


def greet(barrier, me, i):
    pl.semaphore_signal(barrier, inc=1, device_id=place(peer(me, i)), device_id_type=pl.DeviceIdType.MESH)


def send_block(source_ref, target_ref, send_sem, recv_sem, me, number):
    pltpu.make_async_remote_copy(
        src_ref=source_ref.at[number],
        dst_ref=target_ref.at[me],
        send_sem=send_sem,
        recv_sem=recv_sem,
        device_id=place(number),
        device_id_type=pl.DeviceIdType.MESH,
    ).start()


def finish_blocks(source_ref, target_ref, send_sem, recv_sem, me, peers):
    target_ref[me] = source_ref[me]
    rest = pl.ds(0, peers - 1)
    all_of_them = pltpu.make_async_remote_copy(
        src_ref=source_ref.at[rest],
        dst_ref=target_ref.at[rest],
        send_sem=send_sem,
        recv_sem=recv_sem,
        device_id=place(peer(me, 1)),
        device_id_type=pl.DeviceIdType.MESH,
    )
    all_of_them.wait_send()
    all_of_them.wait_recv()


def pack_kernel(
    index_ref, pos_ref, vel_ref, mass_ref, thick_ref, out_ref, rows_ref, stage_ref, send_sem, recv_sem
):
    nodes = pos_ref.shape[1]
    peers = out_ref.shape[0]
    me = my_number()
    barrier = pltpu.get_barrier_semaphore()

    def greet_one(i, carry):
        greet(barrier, me, i)
        return carry

    lax.fori_loop(1, peers, greet_one, 0)

    def fill(b, carry):
        at = pl.ds(pl.multiple_of(b * 128, 128), 128)
        tile = jnp.concatenate([pos_ref[:, at], vel_ref[:, at], mass_ref[:, at], thick_ref[:, at]], axis=0)
        rows_ref[at, :] = expand_rows(tile)
        return carry

    lax.fori_loop(0, nodes // 128, fill, 0, unroll=8)
    rows_ref[nodes : nodes + 8, :] = jnp.zeros((8, 128), F32)
    pl.semaphore_wait(barrier, peers - 1)

    def gather(i):
        number = peer(me, i)
        for part in range(CHUNK // 128):
            lines = []
            for r in range(8):
                got = [rows_ref[pl.ds(index_ref.at[part * 128 + k * 8 + r][number], 1), :] for k in range(16)]
                lines.append(jnp.broadcast_to(merge_groups(got, (1, 128)), (8, 128)))
            stage_ref[number, part] = feature_major(lines)

    def send(i):
        send_block(stage_ref, out_ref, send_sem, recv_sem, me, peer(me, i))

    gather(1)
    gather(2)

    def turn(i, carry):
        send(i - 1)
        gather(i + 1)
        return carry

    lax.fori_loop(2, peers, turn, 0)
    send(peers - 1)
    finish_blocks(stage_ref, out_ref, send_sem, recv_sem, me, peers)


VMEM = pl.BlockSpec(memory_space=pltpu.VMEM)
SMEM = pl.BlockSpec(memory_space=pltpu.SMEM)


def columns(pack_index):
    return pack_index.reshape(-1, CHUNK).T


def pack(positions, velocities, nodal_mass, thickness, pack_index):
    nodes = positions.shape[1]
    blocks = (pack_index.shape[1] // CHUNK, CHUNK // 128, 8, 128)
    return pl.pallas_call(
        pack_kernel,
        out_shape=jax.ShapeDtypeStruct(blocks, F32),
        in_specs=[SMEM, VMEM, VMEM, VMEM, VMEM],
        out_specs=VMEM,
        scratch_shapes=[
            pltpu.VMEM((nodes + 8, 128), F32),
            pltpu.VMEM(blocks, F32),
            pltpu.SemaphoreType.DMA,
            pltpu.SemaphoreType.DMA,
        ],
        compiler_params=pltpu.CompilerParams(vmem_limit_bytes=48 << 20, collective_id=0, has_side_effects=True),
        name="pack",
    )(columns(pack_index), positions, velocities, nodal_mass.reshape(1, -1), thickness.reshape(1, -1))


def scatter_kernel(index_ref, force_ref, out_ref, rows_ref, ex_a, ex_b):
    nodes = out_ref.shape[1]
    chunks = index_ref.shape[1]
    tiles = CHUNK // 128

    def spread(c, ex_ref):
        for part in range(tiles):
            ex_ref[part * 128 : part * 128 + 128] = expand_rows(force_ref[c * tiles + part])

    def place(c, ex_ref):
        for j in range(CHUNK):
            rows_ref[pl.ds(index_ref.at[j][c], 1), :] = ex_ref[j : j + 1, :]

    spread(0, ex_a)

    def turn(i, carry):
        spread(2 * i + 1, ex_b)
        place(2 * i, ex_a)
        spread(jnp.minimum(2 * i + 2, chunks - 1), ex_a)
        place(2 * i + 1, ex_b)
        return carry

    lax.fori_loop(0, chunks // 2, turn, 0)

    def collect(b, carry):
        at = pl.multiple_of(b * 128, 128)
        tiles = [rows_ref[pl.ds(at + k * 8, 8), :] for k in range(16)]
        merged = merge_groups(tiles, (8, 128))
        lines = [jnp.broadcast_to(merged[r : r + 1], (8, 128)) for r in range(8)]
        out_ref[:, pl.ds(at, 128)] = feature_major(lines)[0:3]
        return carry

    lax.fori_loop(0, nodes // 128, collect, 0, unroll=8)


def scatter(force, pack_index, nodes):
    return pl.pallas_call(
        scatter_kernel,
        out_shape=jax.ShapeDtypeStruct((3, nodes), F32),
        in_specs=[SMEM, VMEM],
        out_specs=VMEM,
        scratch_shapes=[
            pltpu.VMEM((nodes + 8, 128), F32),
            pltpu.VMEM((CHUNK, 128), F32),
            pltpu.VMEM((CHUNK, 128), F32),
        ],
        compiler_params=pltpu.CompilerParams(vmem_limit_bytes=48 << 20),
        name="scatter",
    )(columns(pack_index), force)


def merge_lanes(tiles):
    lane = iota((8, 128), 1)
    bit = 1
    while len(tiles) > 1:
        odd = (lane & bit) != 0
        tiles = [jnp.where(odd, tiles[2 * i + 1], tiles[2 * i]) for i in range(len(tiles) // 2)]
        bit *= 2
    return tiles[0]


def pick_lanes(row_of, lanes, table_ref):
    spread = jnp.broadcast_to(lanes, (8, 128))
    return merge_lanes([jnp.take_along_axis(table_ref[row_of(j)], spread, axis=1) for j in range(128)])


def segment_features(c, row_ref, lane_ref, state_ref, out_ref):
    corner = []
    for i in range(4):
        row_of = lambda q: row_ref.at[i * 128 + q][c]
        corner.append(pick_lanes(row_of, lane_ref[pl.ds(i, 1), pl.ds(pl.multiple_of(c * 128, 128), 128)], state_ref))
    total = (corner[0] + corner[1] + corner[2] + corner[3]) * 0.25
    centre = total[0:3]
    d1 = corner[2] - corner[0]
    d2 = corner[3] - corner[1]
    w0 = d1[1:2] * d2[2:3] - d1[2:3] * d2[1:2]
    w1 = d1[2:3] * d2[0:1] - d1[0:1] * d2[2:3]
    w2 = d1[0:1] * d2[1:2] - d1[1:2] * d2[0:1]
    scale = jnp.maximum(jnp.sqrt(w0 * w0 + w1 * w1 + w2 * w2), 1.0)
    off = [corner[i][0:3] - centre for i in range(4)]
    square = off[0] * off[0] + off[1] * off[1] + off[2] * off[2] + off[3] * off[3]
    spread = (square[0:1] + square[1:2] + square[2:3]) * 0.25
    rows = [centre, w0 / scale, w1 / scale, w2 / scale, total[3:6], spread, jnp.zeros((6, 128), F32)]
    out_ref[:, pl.ds(pl.multiple_of(c * 128, 128), 128)] = jnp.concatenate(rows, axis=0)


def corner_rows(connectivity):
    rows = (connectivity >> 7).T.reshape(4, -1, 128)
    rows = jnp.transpose(rows, (0, 2, 1)).reshape(512, -1)
    return jnp.pad(rows, ((0, 0), (0, 128 - rows.shape[1])))


AROUND = [(da, db) for da in (-1, 0, 1) for db in (-1, 0, 1) if (da, db) != (0, 0)]


def ghost_exchange(own_ref, ghost_ref, send_sem, recv_sem):
    wide, narrow = lax.axis_index(WIDE), lax.axis_index(NARROW)
    waits = []
    for k, (da, db) in enumerate(AROUND):
        a, b = wide + da, narrow + db
        inside = (a >= 0) & (a < lax.axis_size(WIDE)) & (b >= 0) & (b < lax.axis_size(NARROW))

        def copy(a=a, b=b, k=k):
            return pltpu.make_async_remote_copy(
                src_ref=own_ref.at[:, pl.ds(0, ghost_ref.shape[2])],
                dst_ref=ghost_ref.at[7 - k],
                send_sem=send_sem.at[k],
                recv_sem=recv_sem.at[7 - k],
                device_id=(a, b),
                device_id_type=pl.DeviceIdType.MESH,
            )

        def arrival(a=a, b=b, k=k):
            return pltpu.make_async_remote_copy(
                src_ref=own_ref.at[:, pl.ds(0, ghost_ref.shape[2])],
                dst_ref=ghost_ref.at[k],
                send_sem=send_sem.at[k],
                recv_sem=recv_sem.at[k],
                device_id=(a, b),
                device_id_type=pl.DeviceIdType.MESH,
            )

        @pl.when(inside)
        def _():
            copy().start()

        @pl.when(jnp.logical_not(inside))
        def _():
            ghost_ref[k] = jnp.zeros(ghost_ref.shape[1:], F32)

        waits.append((inside, arrival))

    def finish():
        for inside, arrival in waits:

            @pl.when(inside)
            def _():
                arrival().wait_send()
                arrival().wait_recv()

    return finish


def contact_kernel(
    tiles_ref,
    entry_ref,
    count_ref,
    row_ref,
    lane_ref,
    state_ref,
    mask_ref,
    out_ref,
    own_ref,
    coef_ref,
    normal_ref,
    keep_a,
    keep_b,
    ghost_ref,
    stage_ref,
    ghost_send,
    ghost_recv,
    send_sem,
    recv_sem,
    *,
    stiffness,
    damping,
):
    blocks = state_ref.shape[0]
    peers = out_ref.shape[0]
    me = my_number()
    barrier = pltpu.get_barrier_semaphore()

    def corners(c, carry):
        segment_features(c, row_ref, lane_ref, state_ref, own_ref)
        return carry

    ghost_chunks = ghost_ref.shape[2] // 128
    first_ones = 1 + (peers - 1) % ghost_chunks
    for i in range(1, first_ones):
        greet(barrier, me, i)
    share = (peers - first_ones) // ghost_chunks

    def corners_and_greet(c, carry):
        for j in range(share):
            greet(barrier, me, first_ones + c * share + j)
        return corners(c, carry)

    lax.fori_loop(0, ghost_chunks, corners_and_greet, 0)
    lax.fori_loop(ghost_chunks, ghost_chunks + 2, corners, 0)
    pl.semaphore_wait(barrier, peers - 1)
    finish_ghosts = ghost_exchange(own_ref, ghost_ref, ghost_send, ghost_recv)
    lax.fori_loop(ghost_chunks + 2, own_ref.shape[1] // 128, corners, 0)

    def prepare(s, f):
        n = f[3:6]
        rate = LOG2E / (f[9:10] + 0.25)
        one = jnp.ones((1, 256), F32)
        zero = jnp.zeros((3, 256), F32)
        dot = lambda a, b: jnp.sum(a * b, axis=0, keepdims=True)
        sides = (
            [-n, dot(f[0:3], n), one],
            [2.0 * rate * f[0:3], -rate * dot(f[0:3], f[0:3]), -rate],
            [-damping * n, damping * dot(f[6:9], n), stiffness * one],
        )
        for i, rows in enumerate(sides):
            high, middle, low = split3(jnp.concatenate(rows + [zero], axis=0))
            coef_ref[s, i] = pack6([high, high, high, middle, middle, low]).T
        high, middle, _ = split3(n)
        gap = zero[0:1]
        normal_ref[s] = jnp.concatenate([high.astype(F32), gap, middle.astype(F32), gap], axis=0)

    own_blocks = own_ref.shape[1] // 256

    def prepare_own(s, carry):
        prepare(s, own_ref[:, pl.ds(pl.multiple_of(s * 256, 256), 256)])
        return carry

    lax.fori_loop(0, own_blocks, prepare_own, 0)
    finish_ghosts()

    def prepare_ghost(k, carry):
        for half in range(2):
            prepare(own_blocks + 2 * k + half, ghost_ref[k, :, 256 * half : 256 * half + 256])
        return carry

    lax.fori_loop(0, ghost_ref.shape[0], prepare_ghost, 0)
    total = count_ref[0]
    row = iota((8, 128), 0)

    def first(block, keep_ref, slot):
        t = entry_ref[block]
        node = state_ref[block]
        sq = jnp.sum(jnp.where(row < 3, node * node, 0.0), axis=0, keepdims=True)
        one = jnp.ones((1, 128), F32)
        zero = jnp.zeros((3, 128), F32)
        sides = (
            [node[0:3], one, node[7:8]],
            [node[0:3], one, sq],
            [node[3:6], one, node[6:7]],
        )
        left = []
        for rows in sides:
            high, middle, low = split3(jnp.concatenate(rows + [zero], axis=0))
            left.append(pack6([high, middle, low, high, middle, high]))
        for half in range(2):
            s = tiles_ref[1, t + half * blocks]
            term = [jnp.dot(coef_ref[s, i], left[i], preferred_element_type=F32) for i in range(3)]
            size = jnp.maximum(term[0], 0.0) * jnp.exp2(term[1]) * term[2]
            top = size.astype(BF16)
            keep_ref[2 * slot + half, 0] = top
            keep_ref[2 * slot + half, 1] = (size - top.astype(F32)).astype(BF16)

    def second(block, keep_ref, slot):
        t = entry_ref[block]
        force = jnp.zeros((8, 128), F32)
        for half in range(2):
            e = t + half * blocks
            live = jnp.where(e < total, 1.0, 0.0)
            mask = mask_ref[pl.ds(e, 1), :].astype(F32) * live
            weights = (normal_ref[tiles_ref[1, e]] * mask).astype(BF16)
            for part in range(2):
                force += jnp.dot(weights, keep_ref[2 * slot + half, part], preferred_element_type=F32)
        return force[0:4] + force[4:8]

    def finish(i, old_ref):
        last = peer(me, i)
        for k in range(GROUP):
            stage_ref[last, k] = second(last * GROUP + k, old_ref, k)

    def step(i, new_ref, old_ref):
        now, last = peer(me, i), peer(me, i - 1)
        for k in range(GROUP):
            first(now * GROUP + k, new_ref, k)
            stage_ref[last, k] = second(last * GROUP + k, old_ref, k)

    def send(i):
        send_block(stage_ref, out_ref, send_sem, recv_sem, me, peer(me, i))

    for k in range(GROUP):
        first(peer(me, 1) * GROUP + k, keep_b, k)
    step(2, keep_a, keep_b)
    step(3, keep_b, keep_a)

    def turn(i, carry):
        send(2 * i - 1)
        send(2 * i)
        step(2 * i + 2, keep_a, keep_b)
        step(2 * i + 3, keep_b, keep_a)
        return carry

    lax.fori_loop(1, peers // 2 - 1, turn, 0)
    send(peers - 3)
    send(peers - 2)
    step(peers, keep_a, keep_b)
    finish(peers, keep_a)
    send(peers - 1)
    finish_blocks(stage_ref, out_ref, send_sem, recv_sem, me, peers)


def pack6(parts):
    return jnp.concatenate([p.astype(F32) for p in parts], axis=0).astype(BF16)


def contact(state, connectivity, tile_list, pair_mask, tile_count):
    blocks = state.shape[0]
    segs = connectivity.shape[0]
    ghosts = segs // 4
    seg_blocks = (segs + 8 * ghosts) // 256
    back = (blocks // GROUP, GROUP, 4, 128)
    number = jnp.arange(blocks, dtype=I32)
    entry = jnp.sum(jnp.where(tile_list[0:1, :blocks] == number[:, None], number[None], 0), axis=1)
    dma = pltpu.SemaphoreType.DMA
    return pl.pallas_call(
        functools.partial(contact_kernel, stiffness=STIFFNESS, damping=DAMPING),
        out_shape=jax.ShapeDtypeStruct(back, F32),
        in_specs=[SMEM, SMEM, SMEM, SMEM, VMEM, VMEM, VMEM],
        out_specs=VMEM,
        scratch_shapes=[
            pltpu.VMEM((16, segs), F32),
            pltpu.VMEM((seg_blocks, 3, 256, 48), BF16),
            pltpu.VMEM((seg_blocks, 8, 256), F32),
            pltpu.VMEM((2 * GROUP, 2, 256, 128), BF16),
            pltpu.VMEM((2 * GROUP, 2, 256, 128), BF16),
            pltpu.VMEM((8, 16, ghosts), F32),
            pltpu.VMEM(back, F32),
            dma((8,)),
            dma((8,)),
            dma,
            dma,
        ],
        compiler_params=pltpu.CompilerParams(vmem_limit_bytes=32 << 20, collective_id=1, has_side_effects=True),
        name="contact",
    )(tile_list, entry, tile_count, corner_rows(connectivity), (connectivity & 127).T, state, pair_mask)


STIFFNESS = 1.0
DAMPING = 0.3
AXES = (WIDE, NARROW)


def on_device(positions, velocities, nodal_mass, thickness, pack_index, connectivity, tile_list, pair_mask, tile_count):
    state = pack(positions, velocities, nodal_mass, thickness, pack_index).reshape(-1, 8, 128)
    force = contact(state, connectivity, tile_list, pair_mask, tile_count)
    return scatter(force.reshape(-1, 4, 128), pack_index, positions.shape[1])


def solution(mesh):
    return jax.shard_map(
        on_device,
        mesh=mesh,
        in_specs=(
            P(None, AXES),
            P(None, AXES),
            P(AXES),
            P(AXES),
            P(AXES, None),
            P(AXES, None),
            P(None, AXES),
            P(AXES, None),
            P(AXES),
        ),
        out_specs=P(None, AXES),
        check_vma=False,
    )
```

```python
import functools
import jax
import jax.numpy as jnp
from jax import lax
from jax.experimental import pallas as pl
from jax.experimental.pallas import tpu as pltpu
from jax.sharding import PartitionSpec as P

F32 = jnp.float32
BF16 = jnp.bfloat16
I32 = jnp.int32
CHUNK = 512
UNR = 1
GROUP = 4
LOG2E = 1.4426950408889634


def iota(shape, axis):
    return lax.broadcasted_iota(I32, shape, axis)


def split3(x):
    high = x.astype(BF16)
    rest = x - high.astype(F32)
    middle = rest.astype(BF16)
    low = (rest - middle.astype(F32)).astype(BF16)
    return high, middle, low


def expand_rows(tile):
    rows = tile.shape[0]
    high, middle, low = split3(tile)
    parts = [high.astype(F32), middle.astype(F32), low.astype(F32)]
    stacked = jnp.concatenate(parts, axis=0).astype(BF16)
    spread = (iota((3 * rows, 128), 0) % rows == iota((3 * rows, 128), 1) % 8).astype(F32).astype(BF16)
    return lax.dot_general(stacked, spread, (((0,), (0,)), ((), ())), preferred_element_type=F32)


def merge_groups(rows, shape):
    lane = iota(shape, 1)
    bit = 8
    while len(rows) > 1:
        odd = (lane & bit) != 0
        rows = [jnp.where(odd, rows[2 * i + 1], rows[2 * i]) for i in range(len(rows) // 2)]
        bit *= 2
    return rows[0]


def feature_major(rows):
    lane = iota((8, 128), 1)
    pick = (lane // 8) * 8 + iota((8, 128), 0)
    out = None
    for r in range(8):
        moved = jnp.take_along_axis(rows[r], pick, axis=1)
        out = moved if out is None else jnp.where(lane % 8 == r, moved, out)
    return out


def index_chunks(index_ref, body):
    def turn(i, carry):
        body(i, lambda k: index_ref.at[k][i])
        return carry

    lax.fori_loop(0, index_ref.shape[1], turn, 0, unroll=UNR)


def merge_lanes(tiles):
    lane = iota((8, 128), 1)
    bit = 1
    while len(tiles) > 1:
        odd = (lane & bit) != 0
        tiles = [jnp.where(odd, tiles[2 * i + 1], tiles[2 * i]) for i in range(len(tiles) // 2)]
        bit *= 2
    return tiles[0]


def pick_lanes(row_of, lanes, table_ref):
    spread = jnp.broadcast_to(lanes, (8, 128))
    return merge_lanes([jnp.take_along_axis(table_ref[row_of(j)], spread, axis=1) for j in range(128)])


WIDE, NARROW = "wide", "narrow"


def my_number():
    return lax.axis_index(WIDE) * lax.axis_size(NARROW) + lax.axis_index(NARROW)


def peer(me, i):
    return lax.rem(me + 37 * i, lax.axis_size(WIDE) * lax.axis_size(NARROW))


def place(number):
    return lax.div(number, lax.axis_size(NARROW)), lax.rem(number, lax.axis_size(NARROW))


def greet(barrier, me, i):
    pl.semaphore_signal(barrier, inc=1, device_id=place(peer(me, i)), device_id_type=pl.DeviceIdType.MESH)


def send_block(source_ref, target_ref, send_sem, recv_sem, me, number):
    pltpu.make_async_remote_copy(
        src_ref=source_ref.at[number],
        dst_ref=target_ref.at[me],
        send_sem=send_sem,
        recv_sem=recv_sem,
        device_id=place(number),
        device_id_type=pl.DeviceIdType.MESH,
    ).start()


def finish_blocks(source_ref, target_ref, send_sem, recv_sem, me, peers):
    target_ref[me] = source_ref[me]
    rest = pl.ds(0, peers - 1)
    all_of_them = pltpu.make_async_remote_copy(
        src_ref=source_ref.at[rest],
        dst_ref=target_ref.at[rest],
        send_sem=send_sem,
        recv_sem=recv_sem,
        device_id=place(peer(me, 1)),
        device_id_type=pl.DeviceIdType.MESH,
    )
    all_of_them.wait_send()
    all_of_them.wait_recv()


def pack_kernel(
    index_ref, pos_ref, vel_ref, mass_ref, thick_ref, out_ref, rows_ref, stage_ref, send_sem, recv_sem
):
    nodes = pos_ref.shape[1]
    peers = out_ref.shape[0]
    me = my_number()
    barrier = pltpu.get_barrier_semaphore()

    def greet_one(i, carry):
        greet(barrier, me, i)
        return carry

    lax.fori_loop(1, peers, greet_one, 0)

    def fill(b, carry):
        at = pl.ds(pl.multiple_of(b * 128, 128), 128)
        tile = jnp.concatenate([pos_ref[:, at], vel_ref[:, at], mass_ref[:, at], thick_ref[:, at]], axis=0)
        rows_ref[at, :] = expand_rows(tile)
        return carry

    lax.fori_loop(0, nodes // 128, fill, 0, unroll=8)
    rows_ref[nodes : nodes + 8, :] = jnp.zeros((8, 128), F32)
    pl.semaphore_wait(barrier, peers - 1)

    def gather(i):
        number = peer(me, i)
        for part in range(CHUNK // 128):
            lines = []
            for r in range(8):
                got = [rows_ref[pl.ds(index_ref.at[part * 128 + k * 8 + r][number], 1), :] for k in range(16)]
                lines.append(jnp.broadcast_to(merge_groups(got, (1, 128)), (8, 128)))
            stage_ref[number, part] = feature_major(lines)

    def send(i):
        send_block(stage_ref, out_ref, send_sem, recv_sem, me, peer(me, i))

    gather(1)
    gather(2)

    def turn(i, carry):
        send(2 * i - 1)
        send(2 * i)
        gather(2 * i + 1)
        gather(2 * i + 2)
        return carry

    lax.fori_loop(1, peers // 2, turn, 0)
    send(peers - 1)
    finish_blocks(stage_ref, out_ref, send_sem, recv_sem, me, peers)


VMEM = pl.BlockSpec(memory_space=pltpu.VMEM)
SMEM = pl.BlockSpec(memory_space=pltpu.SMEM)


def columns(pack_index):
    return pack_index.reshape(-1, CHUNK).T


def pack(positions, velocities, nodal_mass, thickness, pack_index):
    nodes = positions.shape[1]
    blocks = (pack_index.shape[1] // CHUNK, CHUNK // 128, 8, 128)
    return pl.pallas_call(
        pack_kernel,
        out_shape=jax.ShapeDtypeStruct(blocks, F32),
        in_specs=[SMEM, VMEM, VMEM, VMEM, VMEM],
        out_specs=VMEM,
        scratch_shapes=[
            pltpu.VMEM((nodes + 8, 128), F32),
            pltpu.VMEM(blocks, F32),
            pltpu.SemaphoreType.DMA,
            pltpu.SemaphoreType.DMA,
        ],
        compiler_params=pltpu.CompilerParams(vmem_limit_bytes=48 << 20, collective_id=0, has_side_effects=True),
        name="pack",
    )(columns(pack_index), positions, velocities, nodal_mass.reshape(1, -1), thickness.reshape(1, -1))


def scatter_kernel(index_ref, force_ref, out_ref, rows_ref, ex_a, ex_b):
    nodes = out_ref.shape[1]
    chunks = index_ref.shape[1]
    tiles = CHUNK // 128

    def spread(c, ex_ref):
        for part in range(tiles):
            ex_ref[part * 128 : part * 128 + 128] = expand_rows(force_ref[c * tiles + part])

    def place(c, ex_ref):
        for j in range(CHUNK):
            rows_ref[pl.ds(index_ref.at[j][c], 1), :] = ex_ref[j : j + 1, :]

    spread(0, ex_a)

    def turn(i, carry):
        spread(2 * i + 1, ex_b)
        place(2 * i, ex_a)
        spread(jnp.minimum(2 * i + 2, chunks - 1), ex_a)
        place(2 * i + 1, ex_b)
        return carry

    lax.fori_loop(0, chunks // 2, turn, 0)

    def collect(b, carry):
        at = pl.multiple_of(b * 128, 128)
        tiles = [rows_ref[pl.ds(at + k * 8, 8), :] for k in range(16)]
        merged = merge_groups(tiles, (8, 128))
        lines = [jnp.broadcast_to(merged[r : r + 1], (8, 128)) for r in range(8)]
        out_ref[:, pl.ds(at, 128)] = feature_major(lines)[0:3]
        return carry

    lax.fori_loop(0, nodes // 128, collect, 0, unroll=8)


def scatter(force, pack_index, nodes):
    return pl.pallas_call(
        scatter_kernel,
        out_shape=jax.ShapeDtypeStruct((3, nodes), F32),
        in_specs=[SMEM, VMEM],
        out_specs=VMEM,
        scratch_shapes=[
            pltpu.VMEM((nodes + 8, 128), F32),
            pltpu.VMEM((CHUNK, 128), F32),
            pltpu.VMEM((CHUNK, 128), F32),
        ],
        compiler_params=pltpu.CompilerParams(vmem_limit_bytes=48 << 20),
        name="scatter",
    )(columns(pack_index), force)


def merge_lanes(tiles):
    lane = iota((8, 128), 1)
    bit = 1
    while len(tiles) > 1:
        odd = (lane & bit) != 0
        tiles = [jnp.where(odd, tiles[2 * i + 1], tiles[2 * i]) for i in range(len(tiles) // 2)]
        bit *= 2
    return tiles[0]


def pick_lanes(row_of, lanes, table_ref):
    spread = jnp.broadcast_to(lanes, (8, 128))
    return merge_lanes([jnp.take_along_axis(table_ref[row_of(j)], spread, axis=1) for j in range(128)])


def segment_features(c, row_ref, lane_ref, state_ref, out_ref):
    corner = []
    for i in range(4):
        row_of = lambda q: row_ref.at[i * 128 + q][c]
        corner.append(pick_lanes(row_of, lane_ref[pl.ds(i, 1), pl.ds(pl.multiple_of(c * 128, 128), 128)], state_ref))
    total = (corner[0] + corner[1] + corner[2] + corner[3]) * 0.25
    centre = total[0:3]
    d1 = corner[2] - corner[0]
    d2 = corner[3] - corner[1]
    w0 = d1[1:2] * d2[2:3] - d1[2:3] * d2[1:2]
    w1 = d1[2:3] * d2[0:1] - d1[0:1] * d2[2:3]
    w2 = d1[0:1] * d2[1:2] - d1[1:2] * d2[0:1]
    scale = jnp.maximum(jnp.sqrt(w0 * w0 + w1 * w1 + w2 * w2), 1.0)
    off = [corner[i][0:3] - centre for i in range(4)]
    square = off[0] * off[0] + off[1] * off[1] + off[2] * off[2] + off[3] * off[3]
    spread = (square[0:1] + square[1:2] + square[2:3]) * 0.25
    rows = [centre, w0 / scale, w1 / scale, w2 / scale, total[3:6], spread, jnp.zeros((6, 128), F32)]
    out_ref[:, pl.ds(pl.multiple_of(c * 128, 128), 128)] = jnp.concatenate(rows, axis=0)


def corner_rows(connectivity):
    rows = (connectivity >> 7).T.reshape(4, -1, 128)
    rows = jnp.transpose(rows, (0, 2, 1)).reshape(512, -1)
    return jnp.pad(rows, ((0, 0), (0, 128 - rows.shape[1])))


AROUND = [(da, db) for da in (-1, 0, 1) for db in (-1, 0, 1) if (da, db) != (0, 0)]


def ghost_exchange(own_ref, ghost_ref, send_sem, recv_sem):
    wide, narrow = lax.axis_index(WIDE), lax.axis_index(NARROW)
    waits = []
    for k, (da, db) in enumerate(AROUND):
        a, b = wide + da, narrow + db
        inside = (a >= 0) & (a < lax.axis_size(WIDE)) & (b >= 0) & (b < lax.axis_size(NARROW))

        def copy(a=a, b=b, k=k):
            return pltpu.make_async_remote_copy(
                src_ref=own_ref.at[:, pl.ds(0, ghost_ref.shape[2])],
                dst_ref=ghost_ref.at[7 - k],
                send_sem=send_sem.at[k],
                recv_sem=recv_sem.at[7 - k],
                device_id=(a, b),
                device_id_type=pl.DeviceIdType.MESH,
            )

        def arrival(a=a, b=b, k=k):
            return pltpu.make_async_remote_copy(
                src_ref=own_ref.at[:, pl.ds(0, ghost_ref.shape[2])],
                dst_ref=ghost_ref.at[k],
                send_sem=send_sem.at[k],
                recv_sem=recv_sem.at[k],
                device_id=(a, b),
                device_id_type=pl.DeviceIdType.MESH,
            )

        @pl.when(inside)
        def _():
            copy().start()

        @pl.when(jnp.logical_not(inside))
        def _():
            ghost_ref[k] = jnp.zeros(ghost_ref.shape[1:], F32)

        waits.append((inside, arrival))

    def finish():
        for inside, arrival in waits:

            @pl.when(inside)
            def _():
                arrival().wait_send()
                arrival().wait_recv()

    return finish


def contact_kernel(
    tiles_ref,
    entry_ref,
    count_ref,
    row_ref,
    lane_ref,
    state_ref,
    mask_ref,
    out_ref,
    own_ref,
    coef_ref,
    normal_ref,
    keep_a,
    keep_b,
    ghost_ref,
    stage_ref,
    ghost_send,
    ghost_recv,
    send_sem,
    recv_sem,
    *,
    stiffness,
    damping,
):
    blocks = state_ref.shape[0]
    peers = out_ref.shape[0]
    me = my_number()
    barrier = pltpu.get_barrier_semaphore()

    def corners(c, carry):
        segment_features(c, row_ref, lane_ref, state_ref, own_ref)
        return carry

    ghost_chunks = ghost_ref.shape[2] // 128
    first_ones = 1 + (peers - 1) % ghost_chunks
    for i in range(1, first_ones):
        greet(barrier, me, i)
    share = (peers - first_ones) // ghost_chunks

    def corners_and_greet(c, carry):
        for j in range(share):
            greet(barrier, me, first_ones + c * share + j)
        return corners(c, carry)

    lax.fori_loop(0, ghost_chunks, corners_and_greet, 0)
    lax.fori_loop(ghost_chunks, ghost_chunks + 2, corners, 0)
    pl.semaphore_wait(barrier, peers - 1)
    finish_ghosts = ghost_exchange(own_ref, ghost_ref, ghost_send, ghost_recv)
    lax.fori_loop(ghost_chunks + 2, own_ref.shape[1] // 128, corners, 0)

    def prepare(s, f):
        n = f[3:6]
        rate = LOG2E / (f[9:10] + 0.25)
        one = jnp.ones((1, 256), F32)
        zero = jnp.zeros((3, 256), F32)
        dot = lambda a, b: jnp.sum(a * b, axis=0, keepdims=True)
        sides = (
            [-n, dot(f[0:3], n), one],
            [2.0 * rate * f[0:3], -rate * dot(f[0:3], f[0:3]), -rate],
            [-damping * n, damping * dot(f[6:9], n), stiffness * one],
        )
        for i, rows in enumerate(sides):
            high, middle, low = split3(jnp.concatenate(rows + [zero], axis=0))
            coef_ref[s, i] = pack6([high, high, high, middle, middle, low]).T
        high, middle, _ = split3(n)
        gap = zero[0:1]
        normal_ref[s] = jnp.concatenate([high.astype(F32), gap, middle.astype(F32), gap], axis=0)

    own_blocks = own_ref.shape[1] // 256

    def prepare_own(s, carry):
        prepare(s, own_ref[:, pl.ds(pl.multiple_of(s * 256, 256), 256)])
        return carry

    lax.fori_loop(0, own_blocks, prepare_own, 0)
    finish_ghosts()

    def prepare_ghost(k, carry):
        for half in range(2):
            prepare(own_blocks + 2 * k + half, ghost_ref[k, :, 256 * half : 256 * half + 256])
        return carry

    lax.fori_loop(0, ghost_ref.shape[0], prepare_ghost, 0)
    total = count_ref[0]
    row = iota((8, 128), 0)

    def first(block, keep_ref, slot):
        t = entry_ref[block]
        node = state_ref[block]
        sq = jnp.sum(jnp.where(row < 3, node * node, 0.0), axis=0, keepdims=True)
        one = jnp.ones((1, 128), F32)
        zero = jnp.zeros((3, 128), F32)
        sides = (
            [node[0:3], one, node[7:8]],
            [node[0:3], one, sq],
            [node[3:6], one, node[6:7]],
        )
        left = []
        for rows in sides:
            high, middle, low = split3(jnp.concatenate(rows + [zero], axis=0))
            left.append(pack6([high, middle, low, high, middle, high]))
        for half in range(2):
            s = tiles_ref[1, t + half * blocks]
            term = [jnp.dot(coef_ref[s, i], left[i], preferred_element_type=F32) for i in range(3)]
            size = jnp.maximum(term[0], 0.0) * jnp.exp2(term[1]) * term[2]
            top = size.astype(BF16)
            keep_ref[2 * slot + half, 0] = top
            keep_ref[2 * slot + half, 1] = (size - top.astype(F32)).astype(BF16)

    def second(block, keep_ref, slot):
        t = entry_ref[block]
        force = jnp.zeros((8, 128), F32)
        for half in range(2):
            e = t + half * blocks
            live = jnp.where(e < total, 1.0, 0.0)
            mask = mask_ref[pl.ds(e, 1), :].astype(F32) * live
            weights = (normal_ref[tiles_ref[1, e]] * mask).astype(BF16)
            for part in range(2):
                force += jnp.dot(weights, keep_ref[2 * slot + half, part], preferred_element_type=F32)
        return force[0:4] + force[4:8]

    def finish(i, old_ref):
        last = peer(me, i)
        for k in range(GROUP):
            stage_ref[last, k] = second(last * GROUP + k, old_ref, k)

    def step(i, new_ref, old_ref):
        now, last = peer(me, i), peer(me, i - 1)
        for k in range(GROUP):
            first(now * GROUP + k, new_ref, k)
            stage_ref[last, k] = second(last * GROUP + k, old_ref, k)

    def send(i):
        send_block(stage_ref, out_ref, send_sem, recv_sem, me, peer(me, i))

    keep = (keep_a, keep_b)
    for k in range(GROUP):
        first(peer(me, 1) * GROUP + k, keep_b, k)
    for j in range(2, 6):
        step(j, keep[j % 2], keep[1 - j % 2])
    turns = (peers - 6) // 4

    def turn(i, carry):
        for j in range(4):
            send(4 * i + 1 + j)
        for j in range(4):
            step(4 * i + 6 + j, keep[j % 2], keep[1 - j % 2])
        return carry

    lax.fori_loop(0, turns, turn, 0)
    sent = 4 * turns
    for j in range(sent + 1, sent + 5):
        send(j)
    for j in range(sent + 6, peers + 1):
        step(j, keep[j % 2], keep[1 - j % 2])
    finish(peers, keep[peers % 2])
    for j in range(sent + 5, peers):
        send(j)
    finish_blocks(stage_ref, out_ref, send_sem, recv_sem, me, peers)


def pack6(parts):
    return jnp.concatenate([p.astype(F32) for p in parts], axis=0).astype(BF16)


def contact(state, connectivity, tile_list, pair_mask, tile_count):
    blocks = state.shape[0]
    segs = connectivity.shape[0]
    ghosts = segs // 4
    seg_blocks = (segs + 8 * ghosts) // 256
    back = (blocks // GROUP, GROUP, 4, 128)
    number = jnp.arange(blocks, dtype=I32)
    entry = jnp.sum(jnp.where(tile_list[0:1, :blocks] == number[:, None], number[None], 0), axis=1)
    dma = pltpu.SemaphoreType.DMA
    return pl.pallas_call(
        functools.partial(contact_kernel, stiffness=STIFFNESS, damping=DAMPING),
        out_shape=jax.ShapeDtypeStruct(back, F32),
        in_specs=[SMEM, SMEM, SMEM, SMEM, VMEM, VMEM, VMEM],
        out_specs=VMEM,
        scratch_shapes=[
            pltpu.VMEM((16, segs), F32),
            pltpu.VMEM((seg_blocks, 3, 256, 48), BF16),
            pltpu.VMEM((seg_blocks, 8, 256), F32),
            pltpu.VMEM((2 * GROUP, 2, 256, 128), BF16),
            pltpu.VMEM((2 * GROUP, 2, 256, 128), BF16),
            pltpu.VMEM((8, 16, ghosts), F32),
            pltpu.VMEM(back, F32),
            dma((8,)),
            dma((8,)),
            dma,
            dma,
        ],
        compiler_params=pltpu.CompilerParams(vmem_limit_bytes=32 << 20, collective_id=1, has_side_effects=True),
        name="contact",
    )(tile_list, entry, tile_count, corner_rows(connectivity), (connectivity & 127).T, state, pair_mask)


STIFFNESS = 1.0
DAMPING = 0.3
AXES = (WIDE, NARROW)


def on_device(positions, velocities, nodal_mass, thickness, pack_index, connectivity, tile_list, pair_mask, tile_count):
    state = pack(positions, velocities, nodal_mass, thickness, pack_index).reshape(-1, 8, 128)
    force = contact(state, connectivity, tile_list, pair_mask, tile_count)
    return scatter(force.reshape(-1, 4, 128), pack_index, positions.shape[1])


def solution(mesh):
    return jax.shard_map(
        on_device,
        mesh=mesh,
        in_specs=(
            P(None, AXES),
            P(None, AXES),
            P(AXES),
            P(AXES),
            P(AXES, None),
            P(AXES, None),
            P(None, AXES),
            P(AXES, None),
            P(AXES),
        ),
        out_specs=P(None, AXES),
        check_vma=False,
    )
```
